32 devices in a mesh: group: 2 (over y), ctx: 4 (over z), head: 2 (over x), sub: 2 (over core).
Axes of the slice: x: 2, y: 2, z: 4, core: 2. Of those that a mesh axis runs over, the one named last changes fastest.
Arguments:
- q_lin: bfloat16 [2048, 32, 128], P(('group', 'ctx'), ('head', 'sub')), parts along dimension 0, may hold values from -1.796875 to 1.796875
- k_lin: bfloat16 [2048, 32, 128], P(('group', 'ctx'), ('head', 'sub')), parts along dimension 0, may hold values from -1.796875 to 1.796875
- v_lin: bfloat16 [2048, 32, 128], P(('group', 'ctx'), ('head', 'sub')), parts along dimension 0, may hold values from -6 to 6
- decay_log: float32 [2048, 32], P(('group', 'ctx'), ('head', 'sub')), parts along dimension 0, may hold values from -0.7 to 0, as said below
- q_soft: bfloat16 [2048, 32, 128], P(('group', 'ctx'), ('head', 'sub')), parts along dimension 0, may hold values from -8 to 8, as said below
- k_soft: bfloat16 [2048, 8, 128], P(('group', 'ctx'), ('head', 'sub')), parts along dimension 0, may hold values from -8 to 8, as said below
- v_soft: bfloat16 [2048, 8, 128], P(('group', 'ctx'), ('head', 'sub')), parts along dimension 0, may hold values from -6 to 6
- doc_starts: int32 [12], P('group'), parts along dimension 0, may hold values from 0 to 768, as said below
Outputs:
- lin_out: bfloat16 [2048, 32, 128], P(('group', 'ctx'), ('head', 'sub')), parts along dimension 0
- soft_out: bfloat16 [2048, 32, 128], P(('group', 'ctx'), ('head', 'sub')), parts along dimension 0
The draws below stay inside these ranges and needn't reach their ends.
There are 2 independent parts, one for each index of `group`. The reference program is written for one: setup_inputs(seed, part) draws one part's arguments, and reference() takes and returns one part's arrays. A program takes and returns all parts, laid end to end along the dimension named above; each array names one. Nothing has to cross between parts.
Inputs may be any that keep to these rules, and one draw needn't show every extreme that they name: `decay_log`: entries are negative. `q_soft`: entries are at most 8 in magnitude. `k_soft`: entries are at most 8 in magnitude. `doc_starts`: starts never fall and are multiples of 256; equal starts (empty documents) may occur. The first is 0, the last is 768, and all others lie at or after position (3) * 256.
All inputs are finite; a program needn't handle non-finite values.
Results may differ from the reference program's by a relative error of at most 0.0075.
Values may be sent and summed in bfloat16 or wider, within the bound.
No kernel may reach another device: no remote copies, remote signals or barrier semaphores. Data moves between devices by JAX's collectives and lax.ppermute only.
A program may use at most 64 MiB of HBM per device.

```python
import math
import jax
import jax.numpy as jnp
from jax import lax

SLICE_LENGTH = 256
GRAIN = 256
HDIM = 128
QHEADS = 32
KVHEADS = 8
LHEADS = 32
BUNDLE_LENGTH = 1024
NDOCS = 6
N_CTX = 4


def query_key_pair(key):
    base = jax.random.fold_in(key, 101)
    key_a, key_b = jax.random.split(base, 2)
    keys = jnp.clip(1.58 * jax.random.normal(key_a, (BUNDLE_LENGTH, KVHEADS, HDIM), jnp.float32), -8.0, 8.0)
    queries = jnp.clip(1.58 * jax.random.normal(key_b, (BUNDLE_LENGTH, QHEADS, HDIM), jnp.float32), -8.0, 8.0)
    return (queries, keys)


def draw_q_soft(key, part):
    queries, keys = query_key_pair(key)
    return queries.astype(jnp.bfloat16)


def draw_k_soft(key, part):
    queries, keys = query_key_pair(key)
    return keys.astype(jnp.bfloat16)


def draw_decay_log(key, part):
    base = jax.random.fold_in(key, 202)
    key_a, key_b, key_c, key_d, key_e, seed_handle_six, key_g = jax.random.split(base, 7)
    share = 0.5
    quick = jax.random.uniform(key_a, (LHEADS,)) < share
    quick_rate = jnp.exp(jax.random.uniform(key_b, (LHEADS,), jnp.float32, math.log(1.0 / 50.0), math.log(1.0 / 30.0)))
    slow_rate = jnp.exp(jax.random.uniform(key_c, (LHEADS,), jnp.float32, math.log(0.3 / BUNDLE_LENGTH), math.log(0.6 / BUNDLE_LENGTH)))
    forgetting_speed = jnp.where(quick, quick_rate, slow_rate)
    blocks = BUNDLE_LENGTH // SLICE_LENGTH
    segment_scaling = jax.random.uniform(key_d, (blocks, LHEADS), jnp.float32, 0.6, 1.4)
    position_scaling = jax.random.uniform(key_e, (BUNDLE_LENGTH, LHEADS), jnp.float32, 0.7, 1.4)
    slice_locations = jnp.arange(BUNDLE_LENGTH)
    position_groups = jax.random.randint(seed_handle_six, (2,), 0, BUNDLE_LENGTH)
    recursion_level_count = jax.random.uniform(key_g, (2,), jnp.float32, 0.22, 0.6)
    position_group = jnp.sum(jnp.where(slice_locations[:, None] == position_groups[None, :], recursion_level_count[None, :], 0.0), axis=1)
    content_vectors = -(forgetting_speed[None, :] * segment_scaling[slice_locations // SLICE_LENGTH] * position_scaling) - position_group[:, None]
    return content_vectors.astype(jnp.float32)


def draw_doc_starts(key, part):
    base = jax.random.fold_in(key, 303)
    grains = BUNDLE_LENGTH // GRAIN
    lowest = (N_CTX // 2 + 1) * (SLICE_LENGTH // GRAIN)
    picked = jnp.sort(jax.random.randint(base, (NDOCS - 2,), lowest, grains).astype(jnp.int32))
    starts = jnp.concatenate([jnp.zeros((1,), jnp.int32), picked, jnp.full((1,), grains - 1, jnp.int32)])
    return (starts * GRAIN).astype(jnp.int32)


def steps_of(rng, extent, shards, low, top_value):
    def one(position, blocks):
        steps = jax.random.uniform(jax.random.fold_in(jax.random.fold_in(rng, 6), position), (blocks,), jnp.float32, low / len(shards), top_value / len(shards))
        return jnp.repeat(jnp.exp(steps), extent[position] // blocks).reshape((-1,) + (1,) * (len(extent) - position - 1))

    gain = one(*shards[0])
    for cut in shards[1:]:
        gain = gain * one(*cut)
    return gain


def noise(stream_key, dims, spread, bound, cuts=(), kind=jnp.bfloat16):
    loudness = steps_of(stream_key, dims, cuts, -0.22, 0.18) if cuts else 1.0
    values = jax.random.normal(stream_key, dims, jnp.float32) * spread * loudness
    return jnp.minimum(jnp.maximum(values, -bound), bound).astype(kind)


def setup_inputs(seed: int = 0, part: int = 0) -> dict:
    splits = jax.random.split(jax.random.key(seed), 9)
    part_splits = jax.random.split(jax.random.fold_in(splits[8], part), 9)
    return {
        "q_lin": noise(part_splits[0], (BUNDLE_LENGTH, LHEADS, HDIM), 0.3, 1.796875, ((0, 4), (1, 4))),
        "k_lin": noise(part_splits[1], (BUNDLE_LENGTH, LHEADS, HDIM), 0.3, 1.796875, ((0, 4), (1, 4))),
        "v_lin": noise(part_splits[2], (BUNDLE_LENGTH, LHEADS, HDIM), 1.0, 6.0, ((0, 4), (1, 4))),
        "decay_log": draw_decay_log(jax.random.fold_in(jax.random.fold_in(splits[8], part), 71), part),
        "q_soft": draw_q_soft(jax.random.fold_in(jax.random.fold_in(splits[8], part), 71), part),
        "k_soft": draw_k_soft(jax.random.fold_in(jax.random.fold_in(splits[8], part), 71), part),
        "v_soft": noise(part_splits[6], (BUNDLE_LENGTH, KVHEADS, HDIM), 1.0, 6.0, ((0, 4), (1, 4))),
        "doc_starts": draw_doc_starts(jax.random.fold_in(jax.random.fold_in(splits[8], part), 71), part),
    }


def doc_index(slice_locations, doc_starts):
    return lax.optimization_barrier(jnp.sum((doc_starts[None, :] <= slice_locations[:, None]).astype(jnp.int32), axis=1)) - 1

def lightning_block(q_part, k_part, v_part, a_part, state):
    rise = jnp.cumsum(a_part, axis=0)
    q_full = q_part.astype(jnp.float32)
    k_full = k_part.astype(jnp.float32)
    v_full = v_part.astype(jnp.float32)
    scores = jnp.einsum('ihd,jhd->hij', q_full, k_full)
    rows = jnp.arange(q_part.shape[0])
    lower = (rows[:, None] >= rows[None, :])[None]
    gap = rise.T[:, :, None] - rise.T[:, None, :]
    fade = jnp.where(lower, jnp.exp(jnp.where(lower, gap, 0.0)), 0.0)
    inner = lax.optimization_barrier((scores * fade).astype(jnp.bfloat16)).astype(jnp.float32)
    intra = jnp.einsum('hij,jhd->ihd', inner, v_full)
    lead = q_full * jnp.exp(rise)[:, :, None]
    inter = jnp.einsum('ihd,hde->ihe', lead, state, precision=lax.Precision.HIGHEST)
    total = intra + inter
    normed = total * lax.rsqrt(lax.optimization_barrier(jnp.mean(total * total, axis=-1, keepdims=True)) + 1e-06)
    block_decay = rise[-1]
    tail = k_full * jnp.exp(block_decay[None, :] - rise)[:, :, None]
    tail = lax.optimization_barrier(tail.astype(jnp.bfloat16)).astype(jnp.float32)
    local_state = jnp.einsum('jhd,jhe->hde', tail, v_full)
    return (normed.astype(jnp.bfloat16), block_decay, local_state)

def lightning_layer(q_lin, k_lin, v_lin, decay_log, doc_starts):
    blocks = BUNDLE_LENGTH // SLICE_LENGTH
    q_b = q_lin.reshape(blocks, SLICE_LENGTH, LHEADS, HDIM)
    k_b = k_lin.reshape(blocks, SLICE_LENGTH, LHEADS, HDIM)
    v_b = v_lin.reshape(blocks, SLICE_LENGTH, LHEADS, HDIM)
    a_b = decay_log.reshape(blocks, SLICE_LENGTH, LHEADS)
    firsts = jnp.arange(blocks, dtype=jnp.int32) * SLICE_LENGTH
    keep = doc_index(firsts, doc_starts) == doc_index(firsts + SLICE_LENGTH, doc_starts)

    def advance(state, inputs):
        q_part, k_part, v_part, a_part, keep_one = inputs
        normed, block_decay, local_state = lightning_block(q_part, k_part, v_part, a_part, state)
        state_next = jnp.exp(block_decay)[:, None, None] * state + local_state
        state_next = jnp.where(keep_one, state_next, jnp.zeros_like(state_next))
        return (state_next, normed)
    start = jnp.zeros((LHEADS, HDIM, HDIM), jnp.float32)
    last, outputs = lax.scan(advance, start, (q_b, k_b, v_b, a_b, keep))
    return outputs.reshape(BUNDLE_LENGTH, LHEADS, HDIM)

def softmax_layer(q_soft, k_soft, v_soft, doc_starts):
    group = QHEADS // KVHEADS
    scale = 1.0 / math.sqrt(HDIM)
    keys = k_soft.astype(jnp.float32)
    content_vectors = v_soft.astype(jnp.float32)
    slice_locations = jnp.arange(BUNDLE_LENGTH, dtype=jnp.int32)
    key_doc = doc_index(slice_locations, doc_starts)

    def one(block):
        q_part = lax.dynamic_slice_in_dim(q_soft, block * SLICE_LENGTH, SLICE_LENGTH, 0)
        q_part = q_part.astype(jnp.float32).reshape(SLICE_LENGTH, KVHEADS, group, HDIM)
        q_pos = block * SLICE_LENGTH + jnp.arange(SLICE_LENGTH, dtype=jnp.int32)
        q_doc = doc_index(q_pos, doc_starts)
        allowed = (slice_locations[None, :] <= q_pos[:, None]) & (key_doc[None, :] == q_doc[:, None])
        scores = jnp.einsum('tkgd,skd->tkgs', q_part, keys) * scale
        scores = jnp.where(allowed[:, None, None, :], scores, -jnp.inf)
        top = lax.optimization_barrier(jnp.max(scores, axis=-1, keepdims=True))
        weights = jnp.exp(scores - top)
        total = lax.optimization_barrier(jnp.sum(weights, axis=-1))
        rounded = lax.optimization_barrier(weights.astype(jnp.bfloat16)).astype(jnp.float32)
        mixed = jnp.einsum('tkgs,skd->tkgd', rounded, content_vectors) / total[..., None]
        return mixed.reshape(SLICE_LENGTH, QHEADS, HDIM).astype(jnp.bfloat16)
    outputs = lax.map(one, jnp.arange(BUNDLE_LENGTH // SLICE_LENGTH, dtype=jnp.int32))
    return outputs.reshape(BUNDLE_LENGTH, QHEADS, HDIM)

def reference(q_lin, k_lin, v_lin, decay_log, q_soft, k_soft, v_soft, doc_starts):
    lin_out = lightning_layer(q_lin, k_lin, v_lin, decay_log, doc_starts)
    soft_out = softmax_layer(q_soft, k_soft, v_soft, doc_starts)
    return (lin_out, soft_out)
```

```python
import functools
import math

import jax
import jax.numpy as jnp
from jax import lax
from jax.experimental import pallas as pl
from jax.experimental.pallas import tpu as pltpu
from jax.sharding import PartitionSpec as P

F32 = jnp.float32
BF16 = jnp.bfloat16
MASKED = -1e30
VMEM = pl.BlockSpec(memory_space=pltpu.VMEM)
SMEM = pl.BlockSpec(memory_space=pltpu.SMEM)


def call(body, outs, ins, scratch=(), flops=0, name=None):
    moved = sum(math.prod(x.shape) * x.dtype.itemsize for x in list(outs) + [i for i, _ in ins])
    return pl.pallas_call(
        body,
        out_shape=tuple(outs),
        in_specs=[spec for _, spec in ins],
        out_specs=tuple(VMEM for _ in outs),
        scratch_shapes=list(scratch),
        cost_estimate=pl.CostEstimate(flops=flops, bytes_accessed=moved, transcendentals=0),
        name=name,
    )(*[value for value, _ in ins])


def shaped(shape, dtype):
    return jax.ShapeDtypeStruct(shape, dtype)


def rise_of(decay):
    tok = decay.shape[0]
    rows = lax.broadcasted_iota(jnp.int32, (tok, tok), 0)
    columns = lax.broadcasted_iota(jnp.int32, (tok, tok), 1)
    lower = (rows >= columns).astype(F32)
    return jnp.dot(lower, decay, precision=lax.Precision.HIGHEST, preferred_element_type=F32)


def state_body(keep_ref, k_ref, v_ref, a_ref, state_ref, send_ref, decay_ref, wide):
    tok, heads, _ = k_ref.shape
    rise = rise_of(a_ref[...])
    last = rise[tok - 1 : tok, :]
    decay_ref[...] = jnp.exp(last)
    fade = jnp.exp(last - rise)
    wide[0] = k_ref[...].astype(F32)
    wide[1] = v_ref[...].astype(F32)
    keep = keep_ref[0] > 0
    for h in range(heads):
        tail = (wide[0, :, h, :] * fade[:, h : h + 1]).astype(BF16)
        value = wide[1, :, h, :].astype(BF16)
        state = lax.dot_general(
            tail, value, (((0,), (0,)), ((), ())), preferred_element_type=F32
        )
        state_ref[h] = state
        send_ref[h] = jnp.where(keep, state, 0.0).astype(BF16)


def intra_body(q_ref, k_ref, v_ref, a_ref, intra_ref, query_ref, lift_ref, wide):
    tok, heads, _ = k_ref.shape
    rise = rise_of(a_ref[...])
    rise_t = jnp.transpose(rise)
    lift_ref[...] = jnp.exp(rise)
    wide[0] = q_ref[...].astype(F32)
    wide[1] = k_ref[...].astype(F32)
    wide[2] = v_ref[...].astype(F32)
    rows = lax.broadcasted_iota(jnp.int32, (tok, tok), 0)
    columns = lax.broadcasted_iota(jnp.int32, (tok, tok), 1)
    lower = rows >= columns
    for h in range(heads):
        query = wide[0, :, h, :].astype(BF16)
        key = wide[1, :, h, :].astype(BF16)
        value = wide[2, :, h, :].astype(BF16)
        query_ref[h] = query
        scores = lax.dot_general(
            query, key, (((1,), (1,)), ((), ())), preferred_element_type=F32
        )
        gap = jnp.where(lower, rise[:, h : h + 1] - rise_t[h : h + 1, :], MASKED)
        inner = (scores * jnp.exp(gap)).astype(BF16)
        intra_ref[h] = jnp.dot(inner, value, preferred_element_type=F32)


def finish_lin_body(intra_ref, query_ref, lift_ref, state_ref, out_ref, wide):
    heads = query_ref.shape[0]
    for h in range(heads):
        inter = jnp.dot(query_ref[h], state_ref[h], preferred_element_type=F32)
        total = intra_ref[h] + lift_ref[:, h : h + 1] * inter
        mean = jnp.mean(total * total, axis=-1, keepdims=True)
        wide[:, h, :] = total * lax.rsqrt(mean + 1e-06)
    out_ref[...] = wide[...].astype(BF16)


def tile_of(kv_heads, heads, q, k_ref, v_ref, split, bias, causal):
    keys = k_ref.shape[0] // kv_heads
    rows = q.shape[0]
    group = heads // kv_heads
    split[0] = k_ref[...].astype(F32)
    split[1] = v_ref[...].astype(F32)
    head_of_row = (lax.broadcasted_iota(jnp.int32, (rows, 128), 0) % heads) // group
    scores = None
    values = []
    for g in range(kv_heads):
        key = split[0, pl.ds(g, keys, stride=kv_heads), :].astype(BF16)
        values.append(split[1, pl.ds(g, keys, stride=kv_heads), :].astype(BF16))
        part = lax.dot_general(q, key, (((1,), (1,)), ((), ())), preferred_element_type=F32)
        mine = jnp.tile(head_of_row, (1, keys // 128)) == g
        scores = part if g == 0 else jnp.where(mine, part, scores)
    scores = scores * (1.0 / math.sqrt(q.shape[1]))
    if causal:
        position = lax.broadcasted_iota(jnp.int32, (rows, keys), 0) // heads
        column = lax.broadcasted_iota(jnp.int32, (rows, keys), 1)
        scores = jnp.where(column <= position, scores, MASKED)
    else:
        scores = scores + bias
    top = jnp.max(scores, axis=-1, keepdims=True)

    def mix(weights):
        weights = weights.astype(BF16)
        acc = None
        for g in range(kv_heads):
            part = jnp.dot(weights, values[g], preferred_element_type=F32)
            acc = part if g == 0 else jnp.where(head_of_row == g, part, acc)
        ones = jnp.ones((keys, 128), BF16)
        return acc, jnp.dot(weights, ones, preferred_element_type=F32)

    return scores, top, mix


def first_tile_body(kv_heads, heads, q_ref, k_ref, v_ref, top_ref, sum_ref, acc_ref, split):
    scores, top, mix = tile_of(kv_heads, heads, q_ref[...], k_ref, v_ref, split, None, True)
    acc, summed = mix(jnp.exp(scores - top))
    top_ref[...] = jnp.broadcast_to(top, top_ref.shape)
    sum_ref[...] = summed
    acc_ref[...] = acc


def next_tile_body(
    kv_heads, heads, last, bias_ref, q_ref, k_ref, v_ref, top_ref, sum_ref, acc_ref, *rest
):
    scores, top, mix = tile_of(
        kv_heads, heads, q_ref[...], k_ref, v_ref, rest[-1], bias_ref[0], False
    )
    old = top_ref[:, :1]
    new = jnp.maximum(old, top)
    acc, summed = mix(jnp.exp(scores - new))
    shrink = jnp.exp(old - new)
    acc = acc_ref[...] * shrink + acc
    summed = sum_ref[...] * shrink + summed
    if last:
        rest[0][...] = (acc / summed).astype(BF16)
    else:
        rest[0][...] = jnp.broadcast_to(new, top_ref.shape)
        rest[1][...] = summed
        rest[2][...] = acc


def doc_index(position, doc_starts):
    return jnp.sum((doc_starts <= position).astype(jnp.int32)) - 1


def on_device(q_lin, k_lin, v_lin, decay_log, q_soft, k_soft, v_soft, doc_starts):
    tok, heads, dim = q_lin.shape
    soft_heads, kv_heads = (q_soft.shape[1], k_soft.shape[1])
    ranks = lax.axis_size("ctx")
    me = lax.axis_index("ctx")
    here = doc_index(me * tok, doc_starts)
    keep = (here == doc_index((me + 1) * tok, doc_starts)).astype(jnp.int32)[None]

    rows, cols = (tok * soft_heads, tok * kv_heads)
    q = q_soft.reshape(rows, dim)
    held = (k_soft.reshape(cols, dim), v_soft.reshape(cols, dim))
    wide_row = shaped((rows, 128), F32)
    split = pltpu.VMEM((2, cols, dim), F32)
    tile_flops = 6 * rows * tok * dim

    state, send, factor = call(
        state_body,
        (shaped((heads, dim, dim), F32), shaped((heads, dim, dim), BF16), shaped((1, heads), F32)),
        ((keep, SMEM), (k_lin, VMEM), (v_lin, VMEM), (decay_log, VMEM)),
        (pltpu.VMEM((2, tok, heads, dim), F32),),
        flops=2 * heads * tok * dim * dim,
        name="state",
    )
    factor = factor[0][:, None, None]

    stats = call(
        functools.partial(first_tile_body, kv_heads, soft_heads),
        (wide_row, wide_row, wide_row),
        ((q, VMEM), (held[0], VMEM), (held[1], VMEM)),
        (split,),
        flops=tile_flops,
        name="first_tile",
    )
    for step in range(1, ranks - 1):
        pairs = [(i, i + 1) for i in range(step - 1, ranks - 2)]
        held = lax.ppermute(held, "ctx", pairs)
        seen = (me >= step) & (doc_index((me - step) * tok, doc_starts) == here)
        bias = jnp.where(seen, 0.0, MASKED).astype(F32)[None]
        last = step == ranks - 2
        stats = call(
            functools.partial(next_tile_body, kv_heads, soft_heads, last),
            (shaped((rows, dim), BF16),) if last else (wide_row, wide_row, wide_row),
            ((bias, SMEM), (q, VMEM), (held[0], VMEM), (held[1], VMEM))
            + tuple((x, VMEM) for x in stats),
            (split,),
            flops=tile_flops,
            name="last_tile" if last else "next_tile",
        )
    soft_out = stats[0].reshape(q_soft.shape)

    entering = jnp.zeros((heads, dim, dim), BF16)
    for step in range(ranks - 2):
        arrived = lax.ppermute(send, "ctx", [(step, step + 1)])
        entering = jnp.where(me == step + 1, arrived, entering)
        if step < ranks - 3:
            send = jnp.where(keep[0] > 0, factor * arrived.astype(F32) + state, 0.0).astype(BF16)

    intra, query, lift = call(
        intra_body,
        (shaped((heads, tok, dim), F32), shaped((heads, tok, dim), BF16), shaped((tok, heads), F32)),
        ((q_lin, VMEM), (k_lin, VMEM), (v_lin, VMEM), (decay_log, VMEM)),
        (pltpu.VMEM((3, tok, heads, dim), F32),),
        flops=4 * heads * tok * tok * dim,
        name="intra",
    )
    (lin_out,) = call(
        finish_lin_body,
        (shaped((tok, heads, dim), BF16),),
        ((intra, VMEM), (query, VMEM), (lift, VMEM), (entering, VMEM)),
        (pltpu.VMEM((tok, heads, dim), F32),),
        flops=2 * heads * tok * dim * dim,
        name="finish_lin",
    )
    return (lin_out, soft_out)


def solution(mesh):
    wide = P(("group", "ctx"), ("head", "sub"), None)
    return jax.shard_map(
        on_device,
        mesh=mesh,
        in_specs=(wide, wide, wide, P(("group", "ctx"), ("head", "sub")), wide, wide, wide, P("group")),
        out_specs=(wide, wide),
        check_vma=False,
    )
```

```python
import functools
import math

import jax
import jax.numpy as jnp
from jax import lax
from jax.experimental import pallas as pl
from jax.experimental.pallas import tpu as pltpu
from jax.sharding import PartitionSpec as P

F32 = jnp.float32
BF16 = jnp.bfloat16
MASKED = -1e30
LOG2E = 1.0 / math.log(2.0)
VMEM = pl.BlockSpec(memory_space=pltpu.VMEM)
SMEM = pl.BlockSpec(memory_space=pltpu.SMEM)


def shaped(shape, dtype):
    return jax.ShapeDtypeStruct(shape, dtype)


def call(body, outs, ins, scratch=(), flops=0, name=None):
    moved = sum(math.prod(x.shape) * x.dtype.itemsize for x in list(outs) + [i for i, _ in ins])
    return pl.pallas_call(
        body,
        out_shape=tuple(outs),
        in_specs=[spec for _, spec in ins],
        out_specs=tuple(VMEM for _ in outs),
        scratch_shapes=list(scratch),
        cost_estimate=pl.CostEstimate(flops=flops, bytes_accessed=moved, transcendentals=0),
        compiler_params=pltpu.CompilerParams(vmem_limit_bytes=16 << 20),
        name=name,
    )(*[value for value, _ in ins])


def doc_at(docs_ref, position):
    count = jnp.int32(0)
    for i in range(docs_ref.shape[0]):
        count += (docs_ref[i] <= position).astype(jnp.int32)
    return count


def rise_of(decay_t):
    tok = decay_t.shape[1]
    rows = lax.broadcasted_iota(jnp.int32, (tok, tok), 0)
    columns = lax.broadcasted_iota(jnp.int32, (tok, tok), 1)
    upper = (rows <= columns).astype(F32)
    return jnp.dot(decay_t, upper, precision=lax.Precision.HIGHEST, preferred_element_type=F32)


def dot_t(a, b):
    return lax.dot_general(a, b, (((1,), (1,)), ((), ())), preferred_element_type=F32)


def dot(a, b):
    return jnp.dot(a, b, preferred_element_type=F32)


def state_body(me_ref, docs_ref, k_ref, v_ref, a_ref, state_ref, send_ref, factor_ref, kh_ref, vh_ref, kw, vw):
    heads, tok = a_ref.shape
    start = me_ref[0] * tok
    keep = doc_at(docs_ref, start) == doc_at(docs_ref, start + tok)
    rise = rise_of(a_ref[...])
    last = rise[:, tok - 1 : tok]
    factor_ref[...] = jnp.where(keep, jnp.broadcast_to(jnp.exp(last), factor_ref.shape), 0.0)
    fade = jnp.exp(last - rise)
    kw[...] = k_ref[...].astype(F32)
    vw[...] = v_ref[...].astype(F32)
    for h in range(heads):
        key = kw[pl.ds(h, tok, stride=heads), :]
        value = vw[pl.ds(h, tok, stride=heads), :].astype(BF16)
        kh_ref[h] = key.astype(BF16)
        vh_ref[h] = value
        tail_t = (jnp.transpose(key) * fade[h : h + 1, :]).astype(BF16)
        state = jnp.where(keep, dot(tail_t, value), 0.0)
        state_ref[h] = state
        send_ref[h] = state.astype(BF16)


def intra_body(q_ref, kh_ref, vh_ref, a_ref, intra_ref, qh_ref, lift_ref, qw):
    heads, tok = a_ref.shape
    rise_t = rise_of(a_ref[...]) * LOG2E
    rise = jnp.transpose(rise_t)
    lift_ref[...] = jnp.exp2(rise)
    qw[...] = q_ref[...].astype(F32)
    half = tok // 2
    lower = lax.broadcasted_iota(jnp.int32, (half, half), 0) >= lax.broadcasted_iota(
        jnp.int32, (half, half), 1
    )
    for h in range(heads):
        query = qw[pl.ds(h, tok, stride=heads), :].astype(BF16)
        qh_ref[h] = query
        key, value = (kh_ref[h], vh_ref[h])
        column = rise[:, h : h + 1]
        row = rise_t[h : h + 1, :]
        for part in range(2):
            low, high = (part * half, (part + 1) * half)
            scores = dot_t(query[low:high], key[:high])
            gap = column[low:high] - row[:, :high]
            end = jnp.where(lower, gap[:, low:], MASKED)
            gap = jnp.concatenate([gap[:, :low], end], axis=1) if part else end
            inner = (scores * jnp.exp2(gap)).astype(BF16)
            intra_ref[h, low:high] = dot(inner, value[:high])


def finish_lin_body(intra_ref, qh_ref, lift_ref, before_ref, arrived_ref, out_ref, wide):
    heads, tok, dim = qh_ref.shape
    for h in range(heads):
        inter = dot(qh_ref[h], before_ref[h] + arrived_ref[h])
        total = intra_ref[h] + lift_ref[:, h : h + 1] * inter
        mean = jnp.sum(total * total, axis=-1, keepdims=True) * (1.0 / dim)
        wide[pl.ds(h, tok, stride=heads), :] = total * lax.rsqrt(mean + 1e-06)
    out_ref[...] = wide[...].astype(BF16)


def keys_of(ref, wide, count, g):
    keys = ref.shape[0] // count
    if count == 1:
        return ref[...]
    if g == 0:
        wide[...] = ref[...].astype(F32)
    return wide[pl.ds(g, keys, stride=count), :].astype(BF16)


def first_tile_body(kv_heads, heads, q_ref, k_ref, v_ref, qh_ref, top_ref, acc_ref, qw, kw, vw):
    tok = q_ref.shape[0] // heads
    power = LOG2E / math.sqrt(q_ref.shape[1])
    half = tok // 2
    lower = lax.broadcasted_iota(jnp.int32, (half, half), 0) >= lax.broadcasted_iota(
        jnp.int32, (half, half), 1
    )
    qw[...] = q_ref[...].astype(F32)
    ones = jnp.ones((tok, 128), BF16)
    for g in range(kv_heads):
        key = keys_of(k_ref, kw, kv_heads, g)
        value = jnp.concatenate([keys_of(v_ref, vw, kv_heads, g), ones], axis=1)
        for h in range(g * heads // kv_heads, (g + 1) * heads // kv_heads):
            query = qw[pl.ds(h, tok, stride=heads), :].astype(BF16)
            qh_ref[h] = query
            for part in range(2):
                low, high = (part * half, (part + 1) * half)
                scores = dot_t(query[low:high], key[:high])
                end = jnp.where(lower, scores[:, low:], MASKED)
                scores = jnp.concatenate([scores[:, :low], end], axis=1) if part else end
                top = jnp.max(scores, axis=-1, keepdims=True)
                weights = jnp.exp2((scores - top) * power).astype(BF16)
                top_ref[h, low:high] = jnp.broadcast_to(top, (half, 128))
                acc_ref[h, low:high] = dot(weights, value[:high])


def next_tile_body(
    kv_heads, step, last, me_ref, docs_ref, qh_ref, k_ref, v_ref, top_ref, acc_ref, *rest
):
    heads, tok, dim = qh_ref.shape
    kw, vw = rest[-2:]
    power = LOG2E / math.sqrt(dim)
    start = me_ref[0] * tok
    seen = (me_ref[0] >= step) & (doc_at(docs_ref, start - step * tok) == doc_at(docs_ref, start))
    bias = jnp.where(seen, 0.0, MASKED).astype(F32)
    half = tok // 2
    ones = jnp.ones((tok, 128), BF16)
    for g in range(kv_heads):
        key = keys_of(k_ref, kw, kv_heads, g)
        value = jnp.concatenate([keys_of(v_ref, vw, kv_heads, g), ones], axis=1)
        for h in range(g * heads // kv_heads, (g + 1) * heads // kv_heads):
            for part in range(2):
                low, high = (part * half, (part + 1) * half)
                scores = dot_t(qh_ref[h, low:high], key)
                old = top_ref[h, low:high]
                top = jnp.max(scores, axis=-1, keepdims=True) + bias
                new = jnp.maximum(old, jnp.broadcast_to(top, old.shape))
                shift = jnp.tile(new - bias, (1, tok // 128))
                weights = jnp.exp2((scores - shift) * power).astype(BF16)
                shrink = jnp.exp2((old - new) * power)
                both = dot(weights, value)
                acc = acc_ref[h, low:high, :dim] * shrink + both[:, :dim]
                summed = acc_ref[h, low:high, dim:] * shrink + both[:, dim:]
                if last:
                    rest[1][pl.ds(low * heads + h, half, stride=heads), :] = acc / summed
                else:
                    rest[0][h, low:high] = new
                    rest[1][h, low:high, :dim] = acc
                    rest[1][h, low:high, dim:] = summed
    if last:
        rest[0][...] = rest[1][...].astype(BF16)


def on_device(q_lin, k_lin, v_lin, decay_log, q_soft, k_soft, v_soft, doc_starts):
    tok, heads, dim = q_lin.shape
    soft_heads, kv_heads = (q_soft.shape[1], k_soft.shape[1])
    ranks = lax.axis_size("ctx")
    me = lax.axis_index("ctx")[None]
    flat = lambda x: x.reshape(-1, dim)
    q_lin, k_lin, v_lin, q_soft, k_soft, v_soft = map(
        flat, (q_lin, k_lin, v_lin, q_soft, k_soft, v_soft)
    )
    decay_t = decay_log.T
    place = ((me, SMEM), (doc_starts, SMEM))
    wide_lin = pltpu.VMEM(q_lin.shape, F32)
    wide_q = pltpu.VMEM(q_soft.shape, F32)
    wide_k = pltpu.VMEM(k_soft.shape, F32)
    per_head = shaped((heads, tok, dim), BF16)

    state, send, factor, k_heads, v_heads = call(
        state_body,
        (
            shaped((heads, dim, dim), F32),
            shaped((heads, dim, dim), BF16),
            shaped((heads, 128), F32),
            per_head,
            per_head,
        ),
        place + ((k_lin, VMEM), (v_lin, VMEM), (decay_t, VMEM)),
        (wide_lin, wide_lin),
        flops=2 * heads * tok * dim * dim,
        name="state",
    )

    tile_flops = 6 * soft_heads * tok * tok * dim
    stat_shapes = (shaped((soft_heads, tok, 128), F32), shaped((soft_heads, tok, 2 * dim), F32))
    query, *stats = call(
        functools.partial(first_tile_body, kv_heads, soft_heads),
        (shaped((soft_heads, tok, dim), BF16),) + stat_shapes,
        ((q_soft, VMEM), (k_soft, VMEM), (v_soft, VMEM)),
        (wide_q, wide_k, wide_k),
        flops=tile_flops,
        name="first_tile",
    )
    held = (k_soft, v_soft)
    for step in range(1, ranks - 1):
        pairs = [(i, i + 1) for i in range(step - 1, ranks - 2)]
        held = lax.ppermute(held, "ctx", pairs)
        last = step == ranks - 2
        stats = call(
            functools.partial(next_tile_body, kv_heads, step, last),
            (shaped(q_soft.shape, BF16),) if last else stat_shapes,
            place
            + ((query, VMEM), (held[0], VMEM), (held[1], VMEM))
            + tuple((x, VMEM) for x in stats),
            ((wide_q,) if last else ()) + (wide_k, wide_k),
            flops=tile_flops,
            name="last_tile" if last else "next_tile",
        )
    soft_out = stats[0].reshape(tok, soft_heads, dim)

    before = jnp.zeros((heads, dim, dim), BF16)
    arrived = None
    for step in range(ranks - 2):
        if arrived is not None:
            before = before + arrived
            send = (factor[:, None, :] * arrived.astype(F32) + state).astype(BF16)
        arrived = lax.ppermute(send, "ctx", [(step, step + 1)])

    intra, query, lift = call(
        intra_body,
        (shaped((heads, tok, dim), F32), per_head, shaped((tok, heads), F32)),
        ((q_lin, VMEM), (k_heads, VMEM), (v_heads, VMEM), (decay_t, VMEM)),
        (wide_lin,),
        flops=4 * heads * tok * tok * dim,
        name="intra",
    )
    (lin_out,) = call(
        finish_lin_body,
        (shaped(q_lin.shape, BF16),),
        ((intra, VMEM), (query, VMEM), (lift, VMEM), (before, VMEM), (arrived, VMEM)),
        (wide_lin,),
        flops=2 * heads * tok * dim * dim,
        name="finish_lin",
    )
    return (lin_out.reshape(tok, heads, dim), soft_out)


def solution(mesh):
    wide = P(("group", "ctx"), ("head", "sub"), None)
    return jax.shard_map(
        on_device,
        mesh=mesh,
        in_specs=(wide, wide, wide, P(("group", "ctx"), ("head", "sub")), wide, wide, wide, P("group")),
        out_specs=(wide, wide),
        check_vma=False,
    )
```

```python
import functools
import math

import jax
import jax.numpy as jnp
from jax import lax
from jax.experimental import pallas as pl
from jax.experimental.pallas import tpu as pltpu
from jax.sharding import PartitionSpec as P


F32 = jnp.float32
BF16 = jnp.bfloat16
MASKED = -1e30
LOG2E = 1.0 / math.log(2.0)
VMEM = pl.BlockSpec(memory_space=pltpu.VMEM)
SMEM = pl.BlockSpec(memory_space=pltpu.SMEM)
HBM = pl.BlockSpec(memory_space=pltpu.HBM)
DMA = pltpu.SemaphoreType.DMA


def shaped(shape, dtype):
    return jax.ShapeDtypeStruct(shape, dtype)


def call(body, outs, ins, scratch=(), flops=0, out_spec=VMEM):
    moved = sum(math.prod(x.shape) * x.dtype.itemsize for x in list(outs) + [i for i, _ in ins])
    return pl.pallas_call(
        body,
        out_shape=tuple(outs),
        in_specs=[spec for _, spec in ins],
        out_specs=tuple(out_spec for _ in outs),
        scratch_shapes=list(scratch),
        cost_estimate=pl.CostEstimate(flops=flops, bytes_accessed=moved, transcendentals=0),
        compiler_params=pltpu.CompilerParams(vmem_limit_bytes=16 << 20),
    )(*[pltpu.with_memory_space_constraint(x, pltpu.HBM) if spec is HBM else x for x, spec in ins])


def doc_at(docs_ref, position):
    count = jnp.int32(0)
    for i in range(docs_ref.shape[0]):
        count += (docs_ref[i] <= position).astype(jnp.int32)
    return count


def rise_of(decay_t):
    tok = decay_t.shape[1]
    rows = lax.broadcasted_iota(jnp.int32, (tok, tok), 0)
    columns = lax.broadcasted_iota(jnp.int32, (tok, tok), 1)
    upper = (rows <= columns).astype(F32)
    return jnp.dot(decay_t, upper, precision=lax.Precision.HIGHEST, preferred_element_type=F32)


def dot_t(a, b):
    return lax.dot_general(a, b, (((1,), (1,)), ((), ())), preferred_element_type=F32)


def dot(a, b):
    return jnp.dot(a, b, preferred_element_type=F32)


def load_body(me_ref, docs_hbm, k_hbm, v_hbm, a_hbm, kh_ref, vh_ref, rise_ref, flags_ref, docs, kb, vb, ab, kw, vw, sems):
    heads, tok, _ = kh_ref.shape
    copies = [
        pltpu.make_async_copy(src, dst, sems.at[i])
        for i, (src, dst) in enumerate(((docs_hbm, docs), (a_hbm, ab), (k_hbm, kb), (v_hbm, vb)))
    ]
    for copy in copies:
        copy.start()
    copies[0].wait()
    here = me_ref[0]
    doc = doc_at(docs, here * tok)
    keep = doc == doc_at(docs, (here + 1) * tok)
    flags_ref[0:1] = jnp.full((1, 128), jnp.where(keep, 1.0, 0.0), F32)
    for step in range(1, flags_ref.shape[0]):
        seen = (here >= step) & (doc_at(docs, (here - step) * tok) == doc)
        flags_ref[step : step + 1] = jnp.full((1, 128), jnp.where(seen, 0.0, MASKED), F32)
    copies[1].wait()
    rise_ref[...] = rise_of(ab[...])
    for copy, narrow, wide, out in ((copies[2], kb, kw, kh_ref), (copies[3], vb, vw, vh_ref)):
        copy.wait()
        wide[...] = narrow[...].astype(F32)
        for h in range(heads):
            out[h] = wide[pl.ds(h, tok, stride=heads), :].astype(BF16)


def state_body(flags_ref, rise_ref, kh_ref, vh_ref, *rest):
    later = (len(rest) - 4) // 2
    fetched, (state_ref, send_ref, factor_ref), placed = (rest[:later], rest[later : later + 3], rest[later + 3 : -1])
    copies = [
        pltpu.make_async_copy(src, dst, rest[-1].at[i])
        for i, (src, dst) in enumerate(zip(fetched, placed))
    ]
    for copy in copies:
        copy.start()
    heads, tok, _ = kh_ref.shape
    keep = flags_ref[0:1, :]
    rise = rise_ref[...]
    last = rise[:, tok - 1 : tok]
    factor_ref[...] = jnp.broadcast_to(jnp.exp(last), factor_ref.shape) * keep
    fade = jnp.exp(last - rise)
    for h in range(heads):
        tail_t = (jnp.transpose(kh_ref[h].astype(F32)) * fade[h : h + 1, :]).astype(BF16)
        state = dot(tail_t, vh_ref[h]) * keep
        state_ref[h] = state
        send_ref[h] = state.astype(BF16)
    for copy in copies:
        copy.wait()


def intra_body(q_ref, kh_ref, vh_ref, rise_ref, intra_ref, qh_ref, lift_ref, qw):
    heads, tok, dim = kh_ref.shape
    rise_t = rise_ref[...] * LOG2E
    rise = jnp.transpose(rise_t)
    qw[...] = q_ref[...].astype(F32)
    half = tok // 2
    lower = lax.broadcasted_iota(jnp.int32, (half, half), 0) >= lax.broadcasted_iota(
        jnp.int32, (half, half), 1
    )
    for h in range(heads):
        query = qw[pl.ds(h, tok, stride=heads), :].astype(BF16)
        qh_ref[h] = query
        key, value = (kh_ref[h], vh_ref[h])
        column = jnp.broadcast_to(rise[:, h : h + 1], (tok, dim))
        lift_ref[h] = jnp.exp2(column)
        row = rise_t[h : h + 1, :]
        for part in range(2):
            low, high = (part * half, (part + 1) * half)
            scores = dot_t(query[low:high], key[:high])
            side = column[low:high, :half]
            end = jnp.exp2(jnp.where(lower, side - row[:, low:high], MASKED))
            fade = jnp.concatenate([jnp.exp2(side - row[:, :low]), end], axis=1) if part else end
            intra_ref[h, low:high] = dot((scores * fade).astype(BF16), value[:high])


def put_out(wide, narrow, out_hbm, sem, part, parts):
    rows = wide.shape[0] // parts
    here = pl.ds(part * rows, rows)
    narrow[here] = wide[here].astype(BF16)
    copy = pltpu.make_async_copy(narrow.at[here], out_hbm.at[here], sem.at[part])
    copy.start()
    return copy


PARTS = 4


def finish_lin_body(intra_ref, qh_ref, lift_ref, before_ref, arrived_ref, out_ref, wide, narrow, sem):
    heads, tok, dim = qh_ref.shape
    ones = jnp.full((dim, dim), 1.0, BF16)
    size = tok // PARTS
    copies = []
    for part in range(PARTS):
        rows = pl.ds(part * size, size)
        for h in range(heads):
            inter = dot(qh_ref[h, rows], before_ref[h] + arrived_ref[h])
            total = intra_ref[h, rows] + lift_ref[h, rows] * inter
            mean = dot((total * total).astype(BF16), ones) * (1.0 / dim)
            wide[pl.ds(part * size * heads + h, size, stride=heads), :] = total * lax.rsqrt(
                mean + 1e-06
            )
        copies.append(put_out(wide, narrow, out_ref, sem, part, PARTS))
    for copy in copies:
        copy.wait()


def keys_of(ref, wide, count, g):
    keys = ref.shape[0] // count
    if count == 1:
        return ref[...]
    if g == 0:
        wide[...] = ref[...].astype(F32)
    return wide[pl.ds(g, keys, stride=count), :].astype(BF16)


def first_tile_body(kv_heads, heads, q_ref, k_ref, v_ref, qh_ref, top_ref, acc_ref, qw, kw, vw):
    tok = q_ref.shape[0] // heads
    power = LOG2E / math.sqrt(q_ref.shape[1])
    half = tok // 2
    lower = lax.broadcasted_iota(jnp.int32, (half, half), 0) >= lax.broadcasted_iota(
        jnp.int32, (half, half), 1
    )
    qw[...] = q_ref[...].astype(F32)
    ones = jnp.ones((tok, 128), BF16)
    for g in range(kv_heads):
        key = keys_of(k_ref, kw, kv_heads, g)
        value = jnp.concatenate([keys_of(v_ref, vw, kv_heads, g), ones], axis=1)
        for h in range(g * heads // kv_heads, (g + 1) * heads // kv_heads):
            query = qw[pl.ds(h, tok, stride=heads), :].astype(BF16)
            qh_ref[h] = query
            for part in range(2):
                low, high = (part * half, (part + 1) * half)
                scores = dot_t(query[low:high], key[:high])
                end = jnp.where(lower, scores[:, low:], MASKED)
                scores = jnp.concatenate([scores[:, :low], end], axis=1) if part else end
                top = jnp.max(scores, axis=-1, keepdims=True)
                weights = jnp.exp2((scores - top) * power).astype(BF16)
                top_ref[h, low:high] = jnp.broadcast_to(top, (half, 128))
                acc_ref[h, low:high] = dot(weights, value[:high])


def next_tile_body(
    kv_heads, step, last, flags_ref, qh_ref, k_ref, v_ref, top_ref, acc_ref, *rest
):
    heads, tok, dim = qh_ref.shape
    kw, vw = rest[-2:]
    power = LOG2E / math.sqrt(dim)
    bias = flags_ref[step : step + 1, :]
    parts = PARTS if last else 2
    size = tok // parts
    ones = jnp.ones((tok, 128), BF16)
    sides = []
    for g in range(kv_heads):
        value = jnp.concatenate([keys_of(v_ref, vw, kv_heads, g), ones], axis=1)
        sides.append((keys_of(k_ref, kw, kv_heads, g), value))
    copies = []
    for part in range(parts):
        rows = pl.ds(part * size, size)
        for h in range(heads):
            key, value = sides[h * kv_heads // heads]
            scores = dot_t(qh_ref[h, rows], key)
            old = top_ref[h, rows]
            top = jnp.max(scores, axis=-1, keepdims=True) + bias
            new = jnp.maximum(old, top)
            shift = jnp.tile(new - bias, (1, tok // 128))
            weights = jnp.exp2((scores - shift) * power).astype(BF16)
            shrink = jnp.exp2((old - new) * power)
            both = dot(weights, value)
            acc = acc_ref[h, rows, :dim] * shrink + both[:, :dim]
            summed = acc_ref[h, rows, dim:] * shrink + both[:, dim:]
            if last:
                rest[1][pl.ds(part * size * heads + h, size, stride=heads), :] = acc / summed
            else:
                rest[0][h, rows] = new
                rest[1][h, rows, :dim] = acc
                rest[1][h, rows, dim:] = summed
        if last:
            copies.append(put_out(rest[1], rest[2], rest[0], rest[3], part, parts))
    for copy in copies:
        copy.wait()


def on_device(q_lin, k_lin, v_lin, decay_log, q_soft, k_soft, v_soft, doc_starts):
    tok, heads, dim = q_lin.shape
    soft_heads, kv_heads = (q_soft.shape[1], k_soft.shape[1])
    ranks = lax.axis_size("ctx")
    me = lax.axis_index("ctx")[None]
    flat = lambda x: x.reshape(-1, dim)
    q_lin, k_lin, v_lin, q_soft, k_soft, v_soft = map(
        flat, (q_lin, k_lin, v_lin, q_soft, k_soft, v_soft)
    )
    decay_t = decay_log.T
    wide_lin = pltpu.VMEM(q_lin.shape, F32)
    wide_q = pltpu.VMEM(q_soft.shape, F32)
    wide_k = pltpu.VMEM(k_soft.shape, F32)
    flat_lin = pltpu.VMEM(q_lin.shape, BF16)
    per_head = shaped((heads, tok, dim), BF16)

    k_heads, v_heads, rise, flags = call(
        load_body,
        (
            per_head,
            per_head,
            shaped((heads, tok), F32),
            shaped((ranks, 128), F32),
        ),
        ((me, SMEM), (doc_starts, HBM), (k_lin, HBM), (v_lin, HBM), (decay_t, HBM)),
        (
            pltpu.SMEM(doc_starts.shape, jnp.int32),
            flat_lin,
            flat_lin,
            pltpu.VMEM((heads, tok), F32),
            wide_lin,
            wide_lin,
            DMA((4,)),
        ),
    )
    fetched = (q_lin, q_soft, k_soft, v_soft)
    state, send, factor, q_lin_here, q_here, k_here, v_here = call(
        state_body,
        (shaped((heads, dim, dim), F32), shaped((heads, dim, dim), BF16), shaped((heads, 128), F32))
        + tuple(shaped(x.shape, x.dtype) for x in fetched),
        ((flags, VMEM), (rise, VMEM), (k_heads, VMEM), (v_heads, VMEM))
        + tuple((x, HBM) for x in fetched),
        (DMA((4,)),),
        flops=2 * heads * tok * dim * dim,
    )

    tile_flops = 6 * soft_heads * tok * tok * dim
    stat_shapes = (shaped((soft_heads, tok, 128), F32), shaped((soft_heads, tok, 2 * dim), F32))
    soft_query, *stats = call(
        functools.partial(first_tile_body, kv_heads, soft_heads),
        (shaped((soft_heads, tok, dim), BF16),) + stat_shapes,
        ((q_here, VMEM), (k_here, VMEM), (v_here, VMEM)),
        (wide_q, wide_k, wide_k),
        flops=tile_flops,
    )
    keys, values = k_soft, v_soft
    for step in range(1, ranks - 1):
        pairs = [(i, i + 1) for i in range(step - 1, ranks - 2)]
        keys = lax.ppermute(keys, "ctx", pairs)
        values = lax.ppermute(values, "ctx", pairs)
        last = step == ranks - 2
        stats = call(
            functools.partial(next_tile_body, kv_heads, step, last),
            (shaped(q_soft.shape, BF16),) if last else stat_shapes,
            ((flags, VMEM), (soft_query, VMEM), (keys, VMEM), (values, VMEM))
            + tuple((x, VMEM) for x in stats),
            ((wide_q, pltpu.VMEM(q_soft.shape, BF16), DMA((PARTS,))) if last else ())
            + (wide_k, wide_k),
            flops=tile_flops,
            out_spec=HBM if last else VMEM,
        )
    soft_out = stats[0].reshape(tok, soft_heads, dim)

    before = jnp.zeros((heads, dim, dim), BF16)
    arrived = None
    for step in range(1, ranks - 1):
        if arrived is not None:
            before = before + arrived
            send = (factor[:, None, :] * arrived.astype(F32) + state).astype(BF16)
        arrived = lax.ppermute(send, "ctx", [(step - 1, step)])

    intra, lin_query, lift = call(
        intra_body,
        (shaped((heads, tok, dim), F32), per_head, shaped((heads, tok, dim), F32)),
        ((q_lin_here, VMEM), (k_heads, VMEM), (v_heads, VMEM), (rise, VMEM)),
        (wide_lin,),
        flops=4 * heads * tok * tok * dim,
    )
    (lin_out,) = call(
        finish_lin_body,
        (shaped(q_lin.shape, BF16),),
        ((intra, VMEM), (lin_query, VMEM), (lift, VMEM), (before, VMEM), (arrived, VMEM)),
        (wide_lin, flat_lin, DMA((PARTS,))),
        flops=2 * heads * tok * dim * dim,
        out_spec=HBM,
    )
    return (lin_out.reshape(tok, heads, dim), soft_out)


def solution(mesh):
    wide = P(("group", "ctx"), ("head", "sub"), None)

    return jax.shard_map(
        on_device,
        mesh=mesh,
        in_specs=(wide, wide, wide, P(("group", "ctx"), ("head", "sub")), wide, wide, wide, P("group")),
        out_specs=(wide, wide),
        check_vma=False,
    )
```

```python
import functools
import math

import jax
import jax.numpy as jnp
from jax import lax
from jax.experimental import pallas as pl
from jax.experimental.pallas import tpu as pltpu
from jax.sharding import PartitionSpec as P


F32 = jnp.float32
BF16 = jnp.bfloat16
MASKED = -1e30
LOG2E = 1.0 / math.log(2.0)
VMEM = pl.BlockSpec(memory_space=pltpu.VMEM)
SMEM = pl.BlockSpec(memory_space=pltpu.SMEM)
HBM = pl.BlockSpec(memory_space=pltpu.HBM)
DMA = pltpu.SemaphoreType.DMA
HALVES = 2


def shaped(shape, dtype):
    return jax.ShapeDtypeStruct(shape, dtype)


def call(body, outs, ins, scratch=(), flops=0, out_spec=VMEM):
    moved = sum(math.prod(x.shape) * x.dtype.itemsize for x in list(outs) + [i for i, _ in ins])
    return pl.pallas_call(
        body,
        out_shape=tuple(outs),
        in_specs=[spec for _, spec in ins],
        out_specs=tuple(out_spec for _ in outs),
        scratch_shapes=list(scratch),
        cost_estimate=pl.CostEstimate(flops=flops, bytes_accessed=moved, transcendentals=0),
        compiler_params=pltpu.CompilerParams(vmem_limit_bytes=16 << 20),
    )(*[pltpu.with_memory_space_constraint(x, pltpu.HBM) if spec is HBM else x for x, spec in ins])


def doc_at(docs_ref, position):
    count = jnp.int32(0)
    for i in range(docs_ref.shape[0]):
        count += (docs_ref[i] <= position).astype(jnp.int32)
    return count


def rise_of(decay_t):
    tok = decay_t.shape[1]
    rows = lax.broadcasted_iota(jnp.int32, (tok, tok), 0)
    columns = lax.broadcasted_iota(jnp.int32, (tok, tok), 1)
    upper = (rows <= columns).astype(F32)
    return jnp.dot(decay_t, upper, precision=lax.Precision.HIGHEST, preferred_element_type=F32)


def dot_t(a, b):
    return lax.dot_general(a, b, (((1,), (1,)), ((), ())), preferred_element_type=F32)


def dot(a, b):
    return jnp.dot(a, b, preferred_element_type=F32)


def load_body(me_ref, docs_hbm, k_hbm, v_hbm, a_hbm, kh_ref, vh_ref, rise_ref, flags_ref, docs, kb, vb, ab, kw, vw, sems):
    heads, tok, _ = kh_ref.shape
    copies = [
        pltpu.make_async_copy(src, dst, sems.at[i])
        for i, (src, dst) in enumerate(((docs_hbm, docs), (a_hbm, ab), (k_hbm, kb), (v_hbm, vb)))
    ]
    for copy in copies:
        copy.start()
    copies[0].wait()
    here = me_ref[0]
    doc = doc_at(docs, here * tok)
    keep = doc == doc_at(docs, (here + 1) * tok)
    flags_ref[0:1] = jnp.full((1, 128), jnp.where(keep, 1.0, 0.0), F32)
    for step in range(1, flags_ref.shape[0]):
        seen = (here >= step) & (doc_at(docs, (here - step) * tok) == doc)
        flags_ref[step : step + 1] = jnp.full((1, 128), jnp.where(seen, 0.0, MASKED), F32)
    copies[1].wait()
    rise_ref[...] = rise_of(ab[...])
    for copy, narrow, wide, out in ((copies[2], kb, kw, kh_ref), (copies[3], vb, vw, vh_ref)):
        copy.wait()
        wide[...] = narrow[...].astype(F32)
        for h in range(heads):
            out[h] = wide[pl.ds(h, tok, stride=heads), :].astype(BF16)


def state_body(flags_ref, rise_ref, kh_ref, vh_ref, *outs):
    heads, tok, _ = kh_ref.shape
    states, sends, factors = (outs[:HALVES], outs[HALVES : 2 * HALVES], outs[2 * HALVES :])
    keep = flags_ref[0:1, :]
    rise = rise_ref[...]
    last = rise[:, tok - 1 : tok]
    factor = jnp.broadcast_to(jnp.exp(last), (heads, 128)) * keep
    fade = jnp.exp(last - rise)
    size = heads // HALVES
    for half in range(HALVES):
        factors[half][...] = factor[half * size : (half + 1) * size]
        for i in range(size):
            h = half * size + i
            tail_t = (jnp.transpose(kh_ref[h].astype(F32)) * fade[h : h + 1, :]).astype(BF16)
            state = dot(tail_t, vh_ref[h]) * keep
            states[half][i] = state
            sends[half][i] = state.astype(BF16)


def fetch_body(*refs):
    count = len(refs) // 2
    copies = [
        pltpu.make_async_copy(src, dst, refs[-1].at[i])
        for i, (src, dst) in enumerate(zip(refs[:count], refs[count:-1]))
    ]
    for copy in copies:
        copy.start()
    for copy in copies:
        copy.wait()


def intra_body(q_ref, kh_ref, vh_ref, rise_ref, intra_ref, qh_ref, lift_ref, qw):
    heads, tok, dim = kh_ref.shape
    rise_t = rise_ref[...] * LOG2E
    rise = jnp.transpose(rise_t)
    qw[...] = q_ref[...].astype(F32)
    half = tok // 2
    lower = lax.broadcasted_iota(jnp.int32, (half, half), 0) >= lax.broadcasted_iota(
        jnp.int32, (half, half), 1
    )
    for h in range(heads):
        query = qw[pl.ds(h, tok, stride=heads), :].astype(BF16)
        qh_ref[h] = query
        key, value = (kh_ref[h], vh_ref[h])
        column = jnp.broadcast_to(rise[:, h : h + 1], (tok, dim))
        lift_ref[h] = jnp.exp2(column)
        row = rise_t[h : h + 1, :]
        for part in range(2):
            low, high = (part * half, (part + 1) * half)
            scores = dot_t(query[low:high], key[:high])
            side = column[low:high, :half]
            end = jnp.exp2(jnp.where(lower, side - row[:, low:high], MASKED))
            fade = jnp.concatenate([jnp.exp2(side - row[:, :low]), end], axis=1) if part else end
            intra_ref[h, low:high] = dot((scores * fade).astype(BF16), value[:high])


def put_out(wide, narrow, out_hbm, sem, part, parts):
    rows = wide.shape[0] // parts
    here = pl.ds(part * rows, rows)
    narrow[here] = wide[here].astype(BF16)
    copy = pltpu.make_async_copy(narrow.at[here], out_hbm.at[here], sem.at[part])
    copy.start()
    return copy


PARTS = 4


def finish_lin_body(intra_ref, qh_ref, lift_ref, *rest):
    befores, arriveds = (rest[:HALVES], rest[HALVES : 2 * HALVES])
    out_ref, wide, narrow, sem = rest[2 * HALVES :]
    heads, tok, dim = qh_ref.shape
    states = [
        before[i] + arrived[i]
        for before, arrived in zip(befores, arriveds)
        for i in range(heads // HALVES)
    ]
    ones = jnp.full((dim, dim), 1.0, BF16)
    size = tok // PARTS
    copies = []
    for part in range(PARTS):
        rows = pl.ds(part * size, size)
        for h in range(heads):
            inter = dot(qh_ref[h, rows], states[h])
            total = intra_ref[h, rows] + lift_ref[h, rows] * inter
            mean = dot((total * total).astype(BF16), ones) * (1.0 / dim)
            wide[pl.ds(part * size * heads + h, size, stride=heads), :] = total * lax.rsqrt(
                mean + 1e-06
            )
        copies.append(put_out(wide, narrow, out_ref, sem, part, PARTS))
    for copy in copies:
        copy.wait()


def keys_of(ref, wide, count, g):
    keys = ref.shape[0] // count
    if count == 1:
        return ref[...]
    if g == 0:
        wide[...] = ref[...].astype(F32)
    return wide[pl.ds(g, keys, stride=count), :].astype(BF16)


def first_tile_body(kv_heads, heads, q_ref, k_ref, v_ref, qh_ref, top_ref, acc_ref, qw, kw, vw):
    tok = q_ref.shape[0] // heads
    power = LOG2E / math.sqrt(q_ref.shape[1])
    half = tok // 2
    lower = lax.broadcasted_iota(jnp.int32, (half, half), 0) >= lax.broadcasted_iota(
        jnp.int32, (half, half), 1
    )
    qw[...] = q_ref[...].astype(F32)
    ones = jnp.ones((tok, 128), BF16)
    for g in range(kv_heads):
        key = keys_of(k_ref, kw, kv_heads, g)
        value = jnp.concatenate([keys_of(v_ref, vw, kv_heads, g), ones], axis=1)
        for h in range(g * heads // kv_heads, (g + 1) * heads // kv_heads):
            query = qw[pl.ds(h, tok, stride=heads), :].astype(BF16)
            qh_ref[h] = query
            for part in range(2):
                low, high = (part * half, (part + 1) * half)
                scores = dot_t(query[low:high], key[:high])
                end = jnp.where(lower, scores[:, low:], MASKED)
                scores = jnp.concatenate([scores[:, :low], end], axis=1) if part else end
                top = jnp.max(scores, axis=-1, keepdims=True)
                weights = jnp.exp2((scores - top) * power).astype(BF16)
                top_ref[h, low:high] = jnp.broadcast_to(top, (half, 128))
                acc_ref[h, low:high] = dot(weights, value[:high])


def next_tile_body(
    kv_heads, step, last, me_ref, flags_ref, qh_ref, k_ref, v_ref, top_ref, acc_ref, *rest
):
    heads, tok, dim = qh_ref.shape
    kw, vw = rest[-2:]
    power = LOG2E / math.sqrt(dim)
    parts = PARTS if last else 2
    size = tok // parts

    def put(part, h, acc, summed):
        rest[1][pl.ds(part * size * heads + h, size, stride=heads), :] = acc / summed

    @pl.when(me_ref[0] >= step)
    def _():
        bias = flags_ref[step : step + 1, :]
        ones = jnp.ones((tok, 128), BF16)
        sides = []
        for g in range(kv_heads):
            value = jnp.concatenate([keys_of(v_ref, vw, kv_heads, g), ones], axis=1)
            sides.append((keys_of(k_ref, kw, kv_heads, g), value))
        copies = []
        for part in range(parts):
            rows = pl.ds(part * size, size)
            for h in range(heads):
                key, value = sides[h * kv_heads // heads]
                scores = dot_t(qh_ref[h, rows], key)
                old = top_ref[h, rows]
                top = jnp.max(scores, axis=-1, keepdims=True) + bias
                new = jnp.maximum(old, top)
                shift = jnp.tile(new - bias, (1, tok // 128))
                weights = jnp.exp2((scores - shift) * power).astype(BF16)
                shrink = jnp.exp2((old - new) * power)
                both = dot(weights, value)
                acc = acc_ref[h, rows, :dim] * shrink + both[:, :dim]
                summed = acc_ref[h, rows, dim:] * shrink + both[:, dim:]
                if last:
                    put(part, h, acc, summed)
                else:
                    rest[0][h, rows] = new
                    rest[1][h, rows, :dim] = acc
                    rest[1][h, rows, dim:] = summed
            if last:
                copies.append(put_out(rest[1], rest[2], rest[0], rest[3], part, parts))
        for copy in copies:
            copy.wait()

    @pl.when(me_ref[0] < step)
    def _():
        if last:
            copies = []
            for part in range(parts):
                rows = pl.ds(part * size, size)
                for h in range(heads):
                    put(part, h, acc_ref[h, rows, :dim], acc_ref[h, rows, dim:])
                copies.append(put_out(rest[1], rest[2], rest[0], rest[3], part, parts))
            for copy in copies:
                copy.wait()
        else:
            rest[0][...] = top_ref[...]
            rest[1][...] = acc_ref[...]


def on_device(q_lin, k_lin, v_lin, decay_log, q_soft, k_soft, v_soft, doc_starts):
    tok, heads, dim = q_lin.shape
    soft_heads, kv_heads = (q_soft.shape[1], k_soft.shape[1])
    ranks = lax.axis_size("ctx")
    me = lax.axis_index("ctx")[None]
    flat = lambda x: x.reshape(-1, dim)
    q_lin, k_lin, v_lin, q_soft, k_soft, v_soft = map(
        flat, (q_lin, k_lin, v_lin, q_soft, k_soft, v_soft)
    )
    decay_t = decay_log.T
    wide_lin = pltpu.VMEM(q_lin.shape, F32)
    wide_q = pltpu.VMEM(q_soft.shape, F32)
    wide_k = pltpu.VMEM(k_soft.shape, F32)
    flat_lin = pltpu.VMEM(q_lin.shape, BF16)
    per_head = shaped((heads, tok, dim), BF16)

    k_heads, v_heads, rise, flags = call(
        load_body,
        (
            per_head,
            per_head,
            shaped((heads, tok), F32),
            shaped((ranks, 128), F32),
        ),
        ((me, SMEM), (doc_starts, HBM), (k_lin, HBM), (v_lin, HBM), (decay_t, HBM)),
        (
            pltpu.SMEM(doc_starts.shape, jnp.int32),
            flat_lin,
            flat_lin,
            pltpu.VMEM((heads, tok), F32),
            wide_lin,
            wide_lin,
            DMA((4,)),
        ),
    )
    part = heads // HALVES
    outs = call(
        state_body,
        (shaped((part, dim, dim), F32),) * HALVES
        + (shaped((part, dim, dim), BF16),) * HALVES
        + (shaped((part, 128), F32),) * HALVES,
        ((flags, VMEM), (rise, VMEM), (k_heads, VMEM), (v_heads, VMEM)),
        flops=2 * heads * tok * dim * dim,
    )
    states, sends, factors = (outs[:HALVES], list(outs[HALVES : 2 * HALVES]), outs[2 * HALVES :])
    fetched = (q_lin, q_soft, k_soft, v_soft)
    q_lin_here, q_here, k_here, v_here = call(
        fetch_body,
        tuple(shaped(x.shape, x.dtype) for x in fetched),
        tuple((x, HBM) for x in fetched),
        (DMA((len(fetched),)),),
    )

    tile_flops = 6 * soft_heads * tok * tok * dim
    stat_shapes = (shaped((soft_heads, tok, 128), F32), shaped((soft_heads, tok, 2 * dim), F32))
    soft_query, *stats = call(
        functools.partial(first_tile_body, kv_heads, soft_heads),
        (shaped((soft_heads, tok, dim), BF16),) + stat_shapes,
        ((q_here, VMEM), (k_here, VMEM), (v_here, VMEM)),
        (wide_q, wide_k, wide_k),
        flops=tile_flops,
    )
    keys, values = k_soft, v_soft
    for step in range(1, ranks - 1):
        pairs = [(i, i + 1) for i in range(step - 1, ranks - 2)]
        keys = lax.ppermute(keys, "ctx", pairs)
        values = lax.ppermute(values, "ctx", pairs)
        last = step == ranks - 2
        stats = call(
            functools.partial(next_tile_body, kv_heads, step, last),
            (shaped(q_soft.shape, BF16),) if last else stat_shapes,
            ((me, SMEM), (flags, VMEM), (soft_query, VMEM), (keys, VMEM), (values, VMEM))
            + tuple((x, VMEM) for x in stats),
            ((wide_q, pltpu.VMEM(q_soft.shape, BF16), DMA((PARTS,))) if last else ())
            + (wide_k, wide_k),
            flops=tile_flops,
            out_spec=HBM if last else VMEM,
        )
    soft_out = stats[0].reshape(tok, soft_heads, dim)

    befores = [jnp.zeros((part, dim, dim), BF16) for _ in range(HALVES)]
    arrived = [None] * HALVES
    for step in range(1, ranks - 1):
        for half in range(HALVES):
            if step > 1:
                befores[half] = befores[half] + arrived[half]
                moved = factors[half][:, None, :] * arrived[half].astype(F32)
                sends[half] = (moved + states[half]).astype(BF16)
            arrived[half] = lax.ppermute(sends[half], "ctx", [(step - 1, step)])

    intra, lin_query, lift = call(
        intra_body,
        (shaped((heads, tok, dim), F32), per_head, shaped((heads, tok, dim), F32)),
        ((q_lin_here, VMEM), (k_heads, VMEM), (v_heads, VMEM), (rise, VMEM)),
        (wide_lin,),
        flops=4 * heads * tok * tok * dim,
    )
    (lin_out,) = call(
        finish_lin_body,
        (shaped(q_lin.shape, BF16),),
        ((intra, VMEM), (lin_query, VMEM), (lift, VMEM)) + tuple((x, VMEM) for x in befores + arrived),
        (wide_lin, flat_lin, DMA((PARTS,))),
        flops=2 * heads * tok * dim * dim,
        out_spec=HBM,
    )
    return (lin_out.reshape(tok, heads, dim), soft_out)


def solution(mesh):
    wide = P(("group", "ctx"), ("head", "sub"), None)

    return jax.shard_map(
        on_device,
        mesh=mesh,
        in_specs=(wide, wide, wide, P(("group", "ctx"), ("head", "sub")), wide, wide, wide, P("group")),
        out_specs=(wide, wide),
        check_vma=False,
    )
```

```python
import functools
import math

import jax
import jax.numpy as jnp
from jax import lax
from jax.experimental import pallas as pl
from jax.experimental.pallas import tpu as pltpu
from jax.sharding import PartitionSpec as P


F32 = jnp.float32
BF16 = jnp.bfloat16
MASKED = -1e30
LOG2E = 1.0 / math.log(2.0)
VMEM = pl.BlockSpec(memory_space=pltpu.VMEM)
SMEM = pl.BlockSpec(memory_space=pltpu.SMEM)
HBM = pl.BlockSpec(memory_space=pltpu.HBM)
DMA = pltpu.SemaphoreType.DMA
SHARE = 7
HALVES = 2


def shaped(shape, dtype):
    return jax.ShapeDtypeStruct(shape, dtype)


def call(body, outs, ins, scratch=(), flops=0, out_spec=VMEM, aliases={}):
    moved = sum(math.prod(x.shape) * x.dtype.itemsize for x in list(outs) + [i for i, _ in ins])
    return pl.pallas_call(
        body,
        out_shape=tuple(outs),
        in_specs=[spec for _, spec in ins],
        out_specs=out_spec if isinstance(out_spec, tuple) else (out_spec,) * len(outs),
        scratch_shapes=list(scratch),
        input_output_aliases=aliases,
        cost_estimate=pl.CostEstimate(flops=flops, bytes_accessed=moved, transcendentals=0),
        compiler_params=pltpu.CompilerParams(vmem_limit_bytes=16 << 20),
    )(*[pltpu.with_memory_space_constraint(x, pltpu.HBM) if spec is HBM else x for x, spec in ins])


def doc_at(docs_ref, position):
    count = jnp.int32(0)
    for i in range(docs_ref.shape[0]):
        count += (docs_ref[i] <= position).astype(jnp.int32)
    return count


def rise_of(decay_t):
    tok = decay_t.shape[1]
    rows = lax.broadcasted_iota(jnp.int32, (tok, tok), 0)
    columns = lax.broadcasted_iota(jnp.int32, (tok, tok), 1)
    upper = (rows <= columns).astype(F32)
    return jnp.dot(decay_t, upper, precision=lax.Precision.HIGHEST, preferred_element_type=F32)


def dot_t(a, b):
    return lax.dot_general(a, b, (((1,), (1,)), ((), ())), preferred_element_type=F32)


def dot(a, b):
    return jnp.dot(a, b, preferred_element_type=F32)


def pack_body(ranks, me_ref, k_hbm, v_hbm, *rest):
    parts, sems = (rest[:-1], rest[-1])

    @pl.when(me_ref[0] < ranks - 2)
    def _():
        rows = k_hbm.shape[0]
        copies = []
        first = 0
        for part in parts:
            end = first + part.shape[0]
            for i, x in enumerate((k_hbm, v_hbm)):
                low, high = (max(first, i * rows), min(end, (i + 1) * rows))
                if low < high:
                    copies.append(
                        pltpu.make_async_copy(
                            x.at[pl.ds(low - i * rows, high - low)],
                            part.at[pl.ds(low - first, high - low)],
                            sems.at[len(copies)],
                        )
                    )
            first = end
        for copy in copies:
            copy.start()
        for copy in copies:
            copy.wait()


def load_body(me_ref, docs_hbm, a_hbm, k_hbm, v_hbm, *rest):
    later = (len(rest) - 12) // 2
    fetched, (kh_ref, vh_ref, rise_ref, flags_ref), placed = (
        rest[:later],
        rest[later : later + 4],
        rest[later + 4 : 2 * later + 4],
    )
    docs, ab, kb, vb, kw, vw, sems, later_sems = rest[2 * later + 4 :]
    heads, tok, _ = kh_ref.shape
    copies = start_all((docs_hbm, a_hbm, k_hbm, v_hbm), (docs, ab, kb, vb), sems)
    extra = start_all(fetched, placed, later_sems)
    copies[0].wait()
    here = me_ref[0]
    doc = doc_at(docs, here * tok)
    keep = doc == doc_at(docs, (here + 1) * tok)
    flags_ref[0:1] = jnp.full((1, 128), jnp.where(keep, 1.0, 0.0), F32)
    for step in range(1, flags_ref.shape[0]):
        seen = (here >= step) & (doc_at(docs, (here - step) * tok) == doc)
        flags_ref[step : step + 1] = jnp.full((1, 128), jnp.where(seen, 0.0, MASKED), F32)
    copies[1].wait()
    rise_ref[...] = rise_of(ab[...])
    for copy, narrow, wide, out in ((copies[2], kb, kw, kh_ref), (copies[3], vb, vw, vh_ref)):
        copy.wait()
        wide[...] = narrow[...].astype(F32)
        for h in range(heads):
            out[h] = wide[pl.ds(h, tok, stride=heads), :].astype(BF16)
    for copy in extra:
        copy.wait()


def start_all(sources, targets, sems):
    copies = [
        pltpu.make_async_copy(src, dst, sems.at[i])
        for i, (src, dst) in enumerate(zip(sources, targets))
    ]
    for copy in copies:
        copy.start()
    return copies


def state_body(flags_ref, rise_ref, kh_ref, vh_ref, *outs):
    heads, tok, _ = kh_ref.shape
    states, sends, factors = (outs[:HALVES], outs[HALVES : 2 * HALVES], outs[2 * HALVES :])
    keep = flags_ref[0:1, :]
    rise = rise_ref[...]
    last = rise[:, tok - 1 : tok]
    factor = jnp.broadcast_to(jnp.exp(last), (heads, 128)) * keep
    fade = jnp.exp(last - rise)
    size = heads // HALVES
    for half in range(HALVES):
        factors[half][...] = factor[half * size : (half + 1) * size]
        for i in range(size):
            h = half * size + i
            tail_t = (jnp.transpose(kh_ref[h].astype(F32)) * fade[h : h + 1, :]).astype(BF16)
            state = dot(tail_t, vh_ref[h]) * keep
            states[half][i] = state
            sends[half][i] = state.astype(BF16)


def intra_body(q_ref, kh_ref, vh_ref, rise_ref, intra_ref, qh_ref, lift_ref, qw):
    heads, tok, dim = kh_ref.shape
    rise_t = rise_ref[...] * LOG2E
    rise = jnp.transpose(rise_t)
    qw[...] = q_ref[...].astype(F32)
    half = tok // 2
    lower = lax.broadcasted_iota(jnp.int32, (half, half), 0) >= lax.broadcasted_iota(
        jnp.int32, (half, half), 1
    )
    for h in range(heads):
        query = qw[pl.ds(h, tok, stride=heads), :].astype(BF16)
        qh_ref[h] = query
        key, value = (kh_ref[h], vh_ref[h])
        column = jnp.broadcast_to(rise[:, h : h + 1], (tok, dim))
        lift_ref[h] = jnp.exp2(column)
        row = rise_t[h : h + 1, :]
        for part in range(2):
            low, high = (part * half, (part + 1) * half)
            scores = dot_t(query[low:high], key[:high])
            side = column[low:high, :half]
            end = jnp.exp2(jnp.where(lower, side - row[:, low:high], MASKED))
            fade = jnp.concatenate([jnp.exp2(side - row[:, :low]), end], axis=1) if part else end
            intra_ref[h, low:high] = dot((scores * fade).astype(BF16), value[:high])


def put_out(wide, narrow, out_hbm, sem, part, parts):
    rows = wide.shape[0] // parts
    here = pl.ds(part * rows, rows)
    narrow[here] = wide[here].astype(BF16)
    copy = pltpu.make_async_copy(narrow.at[here], out_hbm.at[here], sem.at[part])
    copy.start()
    return copy


PARTS = 4


def finish_body(half, intra_ref, qh_ref, lift_ref, before_ref, arrived_ref, *rest):
    heads, tok, dim = qh_ref.shape
    count = heads // HALVES
    last = half == HALVES - 1
    wide = rest[-3] if last else rest[-1]
    ones = jnp.full((dim, dim), 1.0, BF16)
    size = tok // PARTS
    copies = []
    for part in range(PARTS):
        rows = pl.ds(part * size, size)
        for i in range(count):
            h = half * count + i
            inter = dot(qh_ref[h, rows], before_ref[i] + arrived_ref[i])
            total = intra_ref[h, rows] + lift_ref[h, rows] * inter
            mean = dot((total * total).astype(BF16), ones) * (1.0 / dim)
            wide[pl.ds(part * size * heads + h, size, stride=heads), :] = total * lax.rsqrt(
                mean + 1e-06
            )
        if last:
            copies.append(put_out(wide, rest[-2], rest[-4], rest[-1], part, PARTS))
    for copy in copies:
        copy.wait()


def sides_of(parts, wide, count):
    first = 0
    for part in parts:
        wide[first : first + part.shape[0]] = part[...].astype(F32)
        first += part.shape[0]
    keys = first // (2 * count)
    ones = jnp.ones((keys, 128), BF16)
    sides = []
    for g in range(count):
        key, value = (
            wide[pl.ds(side * (first // 2) + g, keys, stride=count), :].astype(BF16)
            for side in range(2)
        )
        sides.append((key, jnp.concatenate([value, ones], axis=1)))
    return sides


def first_tile_body(kv_heads, heads, q_ref, k_ref, v_ref, qh_ref, top_ref, acc_ref, qw, kvw):
    tok = q_ref.shape[0] // heads
    power = LOG2E / math.sqrt(q_ref.shape[1])
    half = tok // 2
    lower = lax.broadcasted_iota(jnp.int32, (half, half), 0) >= lax.broadcasted_iota(
        jnp.int32, (half, half), 1
    )
    qw[...] = q_ref[...].astype(F32)
    for g, (key, value) in enumerate(sides_of((k_ref, v_ref), kvw, kv_heads)):
        for h in range(g * heads // kv_heads, (g + 1) * heads // kv_heads):
            query = qw[pl.ds(h, tok, stride=heads), :].astype(BF16)
            qh_ref[h] = query
            for part in range(2):
                low, high = (part * half, (part + 1) * half)
                scores = dot_t(query[low:high], key[:high])
                end = jnp.where(lower, scores[:, low:], MASKED)
                scores = jnp.concatenate([scores[:, :low], end], axis=1) if part else end
                top = jnp.max(scores, axis=-1, keepdims=True)
                weights = jnp.exp2((scores - top) * power).astype(BF16)
                top_ref[h, low:high] = jnp.broadcast_to(top, (half, 128))
                acc_ref[h, low:high] = dot(weights, value[:high])


def next_tile_body(
    kv_heads, step, last, me_ref, flags_ref, qh_ref, a_ref, b_ref, top_ref, acc_ref, *rest
):
    heads, tok, dim = qh_ref.shape
    power = LOG2E / math.sqrt(dim)
    parts = PARTS if last else 2
    size = tok // parts

    def put(part, h, acc, summed):
        rest[1][pl.ds(part * size * heads + h, size, stride=heads), :] = acc / summed

    @pl.when(me_ref[0] >= step)
    def _():
        bias = flags_ref[step : step + 1, :]
        sides = sides_of((a_ref, b_ref), rest[-1], kv_heads)
        copies = []
        for part in range(parts):
            rows = pl.ds(part * size, size)
            for h in range(heads):
                key, value = sides[h * kv_heads // heads]
                scores = dot_t(qh_ref[h, rows], key)
                old = top_ref[h, rows]
                top = jnp.max(scores, axis=-1, keepdims=True) + bias
                new = jnp.maximum(old, top)
                shift = jnp.tile(new - bias, (1, tok // 128))
                weights = jnp.exp2((scores - shift) * power).astype(BF16)
                shrink = jnp.exp2((old - new) * power)
                both = dot(weights, value)
                acc = acc_ref[h, rows, :dim] * shrink + both[:, :dim]
                summed = acc_ref[h, rows, dim:] * shrink + both[:, dim:]
                if last:
                    put(part, h, acc, summed)
                else:
                    rest[0][h, rows] = new
                    rest[1][h, rows, :dim] = acc
                    rest[1][h, rows, dim:] = summed
            if last:
                copies.append(put_out(rest[1], rest[2], rest[0], rest[3], part, parts))
        for copy in copies:
            copy.wait()

    @pl.when(me_ref[0] < step)
    def _():
        if last:
            copies = []
            for part in range(parts):
                rows = pl.ds(part * size, size)
                for h in range(heads):
                    put(part, h, acc_ref[h, rows, :dim], acc_ref[h, rows, dim:])
                copies.append(put_out(rest[1], rest[2], rest[0], rest[3], part, parts))
            for copy in copies:
                copy.wait()
        else:
            rest[0][...] = top_ref[...]
            rest[1][...] = acc_ref[...]


def on_device(q_lin, k_lin, v_lin, decay_log, q_soft, k_soft, v_soft, doc_starts):
    tok, heads, dim = q_lin.shape
    soft_heads, kv_heads = (q_soft.shape[1], k_soft.shape[1])
    ranks = lax.axis_size("ctx")
    me = lax.axis_index("ctx")[None]
    flat = lambda x: x.reshape(-1, dim)
    q_lin, k_lin, v_lin, q_soft, k_soft, v_soft = map(
        flat, (q_lin, k_lin, v_lin, q_soft, k_soft, v_soft)
    )
    decay_t = decay_log.T
    wide_lin = pltpu.VMEM(q_lin.shape, F32)
    wide_q = pltpu.VMEM(q_soft.shape, F32)
    wide_kv = pltpu.VMEM((2 * k_soft.shape[0], dim), F32)
    flat_lin = pltpu.VMEM(q_lin.shape, BF16)
    per_head = shaped((heads, tok, dim), BF16)

    fetched = (q_lin, q_soft, k_soft, v_soft)
    total = 2 * k_soft.shape[0]
    early = total * SHARE // 16
    part_a, part_b = call(
        functools.partial(pack_body, ranks),
        (shaped((early, dim), BF16), shaped((total - early, dim), BF16)),
        ((me, SMEM), (k_soft, HBM), (v_soft, HBM)),
        (DMA((4,)),),
    )
    k_heads, v_heads, rise, flags, q_lin_here, q_here, k_here, v_here = call(
        load_body,
        (
            per_head,
            per_head,
            shaped((heads, tok), F32),
            shaped((ranks, 128), F32),
        )
        + tuple(shaped(x.shape, x.dtype) for x in fetched),
        ((me, SMEM),)
        + tuple((x, HBM) for x in (doc_starts, decay_t, k_lin, v_lin) + fetched),
        (
            pltpu.SMEM(doc_starts.shape, jnp.int32),
            pltpu.VMEM((heads, tok), F32),
            flat_lin,
            flat_lin,
            wide_lin,
            wide_lin,
            DMA((4,)),
            DMA((len(fetched),)),
        ),
    )
    part = heads // HALVES
    outs = call(
        state_body,
        (shaped((part, dim, dim), F32),) * HALVES
        + (shaped((part, dim, dim), BF16),) * HALVES
        + (shaped((part, 128), F32),) * HALVES,
        ((flags, VMEM), (rise, VMEM), (k_heads, VMEM), (v_heads, VMEM)),
        flops=2 * heads * tok * dim * dim,
    )
    states, sends, factors = (outs[:HALVES], list(outs[HALVES : 2 * HALVES]), outs[2 * HALVES :])
    tile_flops = 6 * soft_heads * tok * tok * dim
    stat_shapes = (shaped((soft_heads, tok, 128), F32), shaped((soft_heads, tok, 2 * dim), F32))
    soft_query, *stats = call(
        functools.partial(first_tile_body, kv_heads, soft_heads),
        (shaped((soft_heads, tok, dim), BF16),) + stat_shapes,
        ((q_here, VMEM), (k_here, VMEM), (v_here, VMEM)),
        (wide_q, wide_kv),
        flops=tile_flops,
    )
    for step in range(1, ranks - 1):
        pairs = [(i, i + 1) for i in range(step - 1, ranks - 2)]
        part_a = lax.ppermute(part_a, "ctx", pairs)
        part_b = lax.ppermute(part_b, "ctx", pairs)
        last = step == ranks - 2
        stats = call(
            functools.partial(next_tile_body, kv_heads, step, last),
            (shaped(q_soft.shape, BF16),) if last else stat_shapes,
            ((me, SMEM), (flags, VMEM), (soft_query, VMEM), (part_a, VMEM), (part_b, VMEM))
            + tuple((x, VMEM) for x in stats),
            ((wide_q, pltpu.VMEM(q_soft.shape, BF16), DMA((PARTS,))) if last else ())
            + (wide_kv,),
            flops=tile_flops,
            out_spec=HBM if last else VMEM,
        )
    soft_out = stats[0].reshape(tok, soft_heads, dim)

    befores = [jnp.zeros((part, dim, dim), BF16) for _ in range(HALVES)]
    arrived = [None] * HALVES
    for step in range(1, ranks - 1):
        for half in range(HALVES):
            if step > 1:
                befores[half] = befores[half] + arrived[half]
                moved = factors[half][:, None, :] * arrived[half].astype(F32)
                sends[half] = (moved + states[half]).astype(BF16)
            arrived[half] = lax.ppermute(sends[half], "ctx", [(step - 1, step)])

    intra, lin_query, lift = call(
        intra_body,
        (shaped((heads, tok, dim), F32), per_head, shaped((heads, tok, dim), F32)),
        ((q_lin_here, VMEM), (k_heads, VMEM), (v_heads, VMEM), (rise, VMEM)),
        (wide_lin,),
        flops=4 * heads * tok * tok * dim,
    )
    result = ()
    for half in range(HALVES):
        last = half == HALVES - 1
        result = call(
            functools.partial(finish_body, half),
            ((shaped(q_lin.shape, BF16),) if last else ()) + (shaped(q_lin.shape, F32),),
            tuple(
                (x, VMEM)
                for x in (intra, lin_query, lift, befores[half], arrived[half]) + result
            ),
            (flat_lin, DMA((PARTS,))) if last else (),
            flops=2 * part * tok * dim * dim,
            out_spec=(HBM, VMEM) if last else VMEM,
            aliases={5: int(last)} if half else {},
        )
    lin_out = result[0]
    return (lin_out.reshape(tok, heads, dim), soft_out)


def solution(mesh):
    wide = P(("group", "ctx"), ("head", "sub"), None)

    return jax.shard_map(
        on_device,
        mesh=mesh,
        in_specs=(wide, wide, wide, P(("group", "ctx"), ("head", "sub")), wide, wide, wide, P("group")),
        out_specs=(wide, wide),
        check_vma=False,
    )
```

```python
import functools
import math

import jax
import jax.numpy as jnp
from jax import lax
from jax.experimental import pallas as pl
from jax.experimental.pallas import tpu as pltpu
from jax.sharding import PartitionSpec as P


F32 = jnp.float32
BF16 = jnp.bfloat16
MASKED = -1e30
LOG2E = 1.0 / math.log(2.0)
VMEM = pl.BlockSpec(memory_space=pltpu.VMEM)
SMEM = pl.BlockSpec(memory_space=pltpu.SMEM)
HBM = pl.BlockSpec(memory_space=pltpu.HBM)
DMA = pltpu.SemaphoreType.DMA
SHARE = 7
CUTS = (0, 4, 8)
HALVES = len(CUTS) - 1


def shaped(shape, dtype):
    return jax.ShapeDtypeStruct(shape, dtype)


def call(body, outs, ins, scratch=(), flops=0, out_spec=VMEM, aliases={}):
    moved = sum(math.prod(x.shape) * x.dtype.itemsize for x in list(outs) + [i for i, _ in ins])
    return pl.pallas_call(
        body,
        out_shape=tuple(outs),
        in_specs=[spec for _, spec in ins],
        out_specs=out_spec if isinstance(out_spec, tuple) else (out_spec,) * len(outs),
        scratch_shapes=list(scratch),
        input_output_aliases=aliases,
        cost_estimate=pl.CostEstimate(flops=flops, bytes_accessed=moved, transcendentals=0),
        compiler_params=pltpu.CompilerParams(vmem_limit_bytes=16 << 20),
    )(*[pltpu.with_memory_space_constraint(x, pltpu.HBM) if spec is HBM else x for x, spec in ins])


def doc_at(docs_ref, position):
    count = jnp.int32(0)
    for i in range(docs_ref.shape[0]):
        count += (docs_ref[i] <= position).astype(jnp.int32)
    return count


def rise_of(decay_t):
    tok = decay_t.shape[1]
    rows = lax.broadcasted_iota(jnp.int32, (tok, tok), 0)
    columns = lax.broadcasted_iota(jnp.int32, (tok, tok), 1)
    upper = (rows <= columns).astype(F32)
    return jnp.dot(decay_t, upper, precision=lax.Precision.HIGHEST, preferred_element_type=F32)


def dot_t(a, b):
    return lax.dot_general(a, b, (((1,), (1,)), ((), ())), preferred_element_type=F32)


def dot(a, b):
    return jnp.dot(a, b, preferred_element_type=F32)


def pack_body(ranks, me_ref, k_hbm, v_hbm, *rest):
    parts, sems = (rest[:-1], rest[-1])

    @pl.when(me_ref[0] < ranks - 2)
    def _():
        rows = k_hbm.shape[0]
        copies = []
        first = 0
        for part in parts:
            end = first + part.shape[0]
            for i, x in enumerate((k_hbm, v_hbm)):
                low, high = (max(first, i * rows), min(end, (i + 1) * rows))
                if low < high:
                    copies.append(
                        pltpu.make_async_copy(
                            x.at[pl.ds(low - i * rows, high - low)],
                            part.at[pl.ds(low - first, high - low)],
                            sems.at[len(copies)],
                        )
                    )
            first = end
        for copy in copies:
            copy.start()
        for copy in copies:
            copy.wait()


def load_body(me_ref, docs_hbm, a_hbm, k_hbm, v_hbm, *rest):
    later = (len(rest) - 12) // 2
    fetched, (kh_ref, vh_ref, rise_ref, flags_ref), placed = (
        rest[:later],
        rest[later : later + 4],
        rest[later + 4 : 2 * later + 4],
    )
    docs, ab, kb, vb, kw, vw, sems, later_sems = rest[2 * later + 4 :]
    heads, tok, _ = kh_ref.shape
    copies = start_all((docs_hbm, a_hbm, k_hbm, v_hbm), (docs, ab, kb, vb), sems)
    extra = start_all(fetched, placed, later_sems)
    copies[0].wait()
    here = me_ref[0]
    doc = doc_at(docs, here * tok)
    keep = doc == doc_at(docs, (here + 1) * tok)
    flags_ref[0:1] = jnp.full((1, 128), jnp.where(keep, 1.0, 0.0), F32)
    for step in range(1, flags_ref.shape[0]):
        seen = (here >= step) & (doc_at(docs, (here - step) * tok) == doc)
        flags_ref[step : step + 1] = jnp.full((1, 128), jnp.where(seen, 0.0, MASKED), F32)
    copies[1].wait()
    rise_ref[...] = rise_of(ab[...])
    for copy, narrow, wide, out in ((copies[2], kb, kw, kh_ref), (copies[3], vb, vw, vh_ref)):
        copy.wait()
        wide[...] = narrow[...].astype(F32)
        for h in range(heads):
            out[h] = wide[pl.ds(h, tok, stride=heads), :].astype(BF16)
    for copy in extra:
        copy.wait()


def start_all(sources, targets, sems):
    copies = [
        pltpu.make_async_copy(src, dst, sems.at[i])
        for i, (src, dst) in enumerate(zip(sources, targets))
    ]
    for copy in copies:
        copy.start()
    return copies


def state_body(flags_ref, rise_ref, kh_ref, vh_ref, *outs):
    heads, tok, _ = kh_ref.shape
    states, sends, factors = (outs[:HALVES], outs[HALVES : 2 * HALVES], outs[2 * HALVES :])
    keep = flags_ref[0:1, :]
    rise = rise_ref[...]
    last = rise[:, tok - 1 : tok]
    factor = jnp.broadcast_to(jnp.exp(last), (heads, 128)) * keep
    fade = jnp.exp(last - rise)
    for half in range(HALVES):
        first, size = group_of(half, heads)
        factors[half][...] = factor[first : first + size]
        for i in range(size):
            h = first + i
            tail_t = (jnp.transpose(kh_ref[h].astype(F32)) * fade[h : h + 1, :]).astype(BF16)
            state = dot(tail_t, vh_ref[h]) * keep
            states[half][i] = state
            sends[half][i] = state.astype(BF16)


def intra_body(q_ref, kh_ref, vh_ref, rise_ref, intra_ref, qh_ref, lift_ref, qw):
    heads, tok, dim = kh_ref.shape
    rise_t = rise_ref[...] * LOG2E
    rise = jnp.transpose(rise_t)
    qw[...] = q_ref[...].astype(F32)
    half = tok // 2
    lower = lax.broadcasted_iota(jnp.int32, (half, half), 0) >= lax.broadcasted_iota(
        jnp.int32, (half, half), 1
    )
    for h in range(heads):
        query = qw[pl.ds(h, tok, stride=heads), :].astype(BF16)
        qh_ref[h] = query
        key, value = (kh_ref[h], vh_ref[h])
        column = jnp.broadcast_to(rise[:, h : h + 1], (tok, dim))
        lift_ref[h] = jnp.exp2(column)
        row = rise_t[h : h + 1, :]
        for part in range(2):
            low, high = (part * half, (part + 1) * half)
            scores = dot_t(query[low:high], key[:high])
            side = column[low:high, :half]
            end = jnp.exp2(jnp.where(lower, side - row[:, low:high], MASKED))
            fade = jnp.concatenate([jnp.exp2(side - row[:, :low]), end], axis=1) if part else end
            intra_ref[h, low:high] = dot((scores * fade).astype(BF16), value[:high])


def put_out(wide, narrow, out_hbm, sem, part, parts):
    rows = wide.shape[0] // parts
    here = pl.ds(part * rows, rows)
    narrow[here] = wide[here].astype(BF16)
    copy = pltpu.make_async_copy(narrow.at[here], out_hbm.at[here], sem.at[part])
    copy.start()
    return copy


PARTS = 2


def group_of(half, heads):
    low, high = (CUTS[half] * heads // 8, CUTS[half + 1] * heads // 8)
    return low, high - low


def finish_body(half, intra_ref, qh_ref, lift_ref, before_ref, arrived_ref, *rest):
    heads, tok, dim = qh_ref.shape
    first, count = group_of(half, heads)
    last = half == HALVES - 1
    wide = rest[-3] if last else rest[-1]
    ones = jnp.full((dim, dim), 1.0, BF16)
    size = tok // PARTS
    copies = []
    for part in range(PARTS):
        rows = pl.ds(part * size, size)
        for i in range(count):
            h = first + i
            inter = dot(qh_ref[h, rows], before_ref[i] + arrived_ref[i])
            total = intra_ref[h, rows] + lift_ref[h, rows] * inter
            mean = dot((total * total).astype(BF16), ones) * (1.0 / dim)
            wide[pl.ds(part * size * heads + h, size, stride=heads), :] = total * lax.rsqrt(
                mean + 1e-06
            )
        if last:
            copies.append(put_out(wide, rest[-2], rest[-4], rest[-1], part, PARTS))
    for copy in copies:
        copy.wait()


def sides_of(parts, wide, count):
    first = 0
    for part in parts:
        wide[first : first + part.shape[0]] = part[...].astype(F32)
        first += part.shape[0]
    keys = first // (2 * count)
    ones = jnp.ones((keys, 128), BF16)
    sides = []
    for g in range(count):
        key, value = (
            wide[pl.ds(side * (first // 2) + g, keys, stride=count), :].astype(BF16)
            for side in range(2)
        )
        sides.append((key, jnp.concatenate([value, ones], axis=1)))
    return sides


def first_tile_body(kv_heads, heads, q_ref, k_ref, v_ref, qh_ref, top_ref, acc_ref, qw, kvw):
    tok = q_ref.shape[0] // heads
    power = LOG2E / math.sqrt(q_ref.shape[1])
    half = tok // 2
    lower = lax.broadcasted_iota(jnp.int32, (half, half), 0) >= lax.broadcasted_iota(
        jnp.int32, (half, half), 1
    )
    qw[...] = q_ref[...].astype(F32)
    for g, (key, value) in enumerate(sides_of((k_ref, v_ref), kvw, kv_heads)):
        for h in range(g * heads // kv_heads, (g + 1) * heads // kv_heads):
            query = qw[pl.ds(h, tok, stride=heads), :].astype(BF16)
            qh_ref[h] = query
            for part in range(2):
                low, high = (part * half, (part + 1) * half)
                scores = dot_t(query[low:high], key[:high])
                end = jnp.where(lower, scores[:, low:], MASKED)
                scores = jnp.concatenate([scores[:, :low], end], axis=1) if part else end
                top = jnp.max(scores, axis=-1, keepdims=True)
                weights = jnp.exp2((scores - top) * power).astype(BF16)
                top_ref[h, low:high] = jnp.broadcast_to(top, (half, 128))
                acc_ref[h, low:high] = dot(weights, value[:high])


def next_tile_body(
    kv_heads, step, last, me_ref, flags_ref, qh_ref, a_ref, b_ref, top_ref, acc_ref, *rest
):
    heads, tok, dim = qh_ref.shape
    power = LOG2E / math.sqrt(dim)
    parts = PARTS if last else 2
    size = tok // parts

    def put(part, h, acc, summed):
        rest[1][pl.ds(part * size * heads + h, size, stride=heads), :] = acc / summed

    @pl.when(me_ref[0] >= step)
    def _():
        bias = flags_ref[step : step + 1, :]
        sides = sides_of((a_ref, b_ref), rest[-1], kv_heads)
        copies = []
        for part in range(parts):
            rows = pl.ds(part * size, size)
            for h in range(heads):
                key, value = sides[h * kv_heads // heads]
                scores = dot_t(qh_ref[h, rows], key)
                old = top_ref[h, rows]
                top = jnp.max(scores, axis=-1, keepdims=True) + bias
                new = jnp.maximum(old, top)
                shift = jnp.tile(new - bias, (1, tok // 128))
                weights = jnp.exp2((scores - shift) * power).astype(BF16)
                shrink = jnp.exp2((old - new) * power)
                both = dot(weights, value)
                acc = acc_ref[h, rows, :dim] * shrink + both[:, :dim]
                summed = acc_ref[h, rows, dim:] * shrink + both[:, dim:]
                if last:
                    put(part, h, acc, summed)
                else:
                    rest[0][h, rows] = new
                    rest[1][h, rows, :dim] = acc
                    rest[1][h, rows, dim:] = summed
            if last:
                copies.append(put_out(rest[1], rest[2], rest[0], rest[3], part, parts))
        for copy in copies:
            copy.wait()

    @pl.when(me_ref[0] < step)
    def _():
        if last:
            copies = []
            for part in range(parts):
                rows = pl.ds(part * size, size)
                for h in range(heads):
                    put(part, h, acc_ref[h, rows, :dim], acc_ref[h, rows, dim:])
                copies.append(put_out(rest[1], rest[2], rest[0], rest[3], part, parts))
            for copy in copies:
                copy.wait()
        else:
            rest[0][...] = top_ref[...]
            rest[1][...] = acc_ref[...]


def on_device(q_lin, k_lin, v_lin, decay_log, q_soft, k_soft, v_soft, doc_starts):
    tok, heads, dim = q_lin.shape
    soft_heads, kv_heads = (q_soft.shape[1], k_soft.shape[1])
    ranks = lax.axis_size("ctx")
    me = lax.axis_index("ctx")[None]
    flat = lambda x: x.reshape(-1, dim)
    q_lin, k_lin, v_lin, q_soft, k_soft, v_soft = map(
        flat, (q_lin, k_lin, v_lin, q_soft, k_soft, v_soft)
    )
    decay_t = decay_log.T
    wide_lin = pltpu.VMEM(q_lin.shape, F32)
    wide_q = pltpu.VMEM(q_soft.shape, F32)
    wide_kv = pltpu.VMEM((2 * k_soft.shape[0], dim), F32)
    flat_lin = pltpu.VMEM(q_lin.shape, BF16)
    per_head = shaped((heads, tok, dim), BF16)

    fetched = (q_lin, q_soft, k_soft, v_soft)
    total = 2 * k_soft.shape[0]
    early = total * SHARE // 16
    part_a, part_b = call(
        functools.partial(pack_body, ranks),
        (shaped((early, dim), BF16), shaped((total - early, dim), BF16)),
        ((me, SMEM), (k_soft, HBM), (v_soft, HBM)),
        (DMA((4,)),),
    )
    k_heads, v_heads, rise, flags, q_lin_here, q_here, k_here, v_here = call(
        load_body,
        (
            per_head,
            per_head,
            shaped((heads, tok), F32),
            shaped((ranks, 128), F32),
        )
        + tuple(shaped(x.shape, x.dtype) for x in fetched),
        ((me, SMEM),)
        + tuple((x, HBM) for x in (doc_starts, decay_t, k_lin, v_lin) + fetched),
        (
            pltpu.SMEM(doc_starts.shape, jnp.int32),
            pltpu.VMEM((heads, tok), F32),
            flat_lin,
            flat_lin,
            wide_lin,
            wide_lin,
            DMA((4,)),
            DMA((len(fetched),)),
        ),
    )
    counts = [group_of(half, heads)[1] for half in range(HALVES)]
    outs = call(
        state_body,
        tuple(shaped((count, dim, dim), F32) for count in counts)
        + tuple(shaped((count, dim, dim), BF16) for count in counts)
        + tuple(shaped((count, 128), F32) for count in counts),
        ((flags, VMEM), (rise, VMEM), (k_heads, VMEM), (v_heads, VMEM)),
        flops=2 * heads * tok * dim * dim,
    )
    states, sends, factors = (outs[:HALVES], list(outs[HALVES : 2 * HALVES]), outs[2 * HALVES :])
    tile_flops = 6 * soft_heads * tok * tok * dim
    stat_shapes = (shaped((soft_heads, tok, 128), F32), shaped((soft_heads, tok, 2 * dim), F32))
    soft_query, *stats = call(
        functools.partial(first_tile_body, kv_heads, soft_heads),
        (shaped((soft_heads, tok, dim), BF16),) + stat_shapes,
        ((q_here, VMEM), (k_here, VMEM), (v_here, VMEM)),
        (wide_q, wide_kv),
        flops=tile_flops,
    )
    for step in range(1, ranks - 1):
        pairs = [(i, i + 1) for i in range(step - 1, ranks - 2)]
        part_a = lax.ppermute(part_a, "ctx", pairs)
        part_b = lax.ppermute(part_b, "ctx", pairs)
        last = step == ranks - 2
        stats = call(
            functools.partial(next_tile_body, kv_heads, step, last),
            (shaped(q_soft.shape, BF16),) if last else stat_shapes,
            ((me, SMEM), (flags, VMEM), (soft_query, VMEM), (part_a, VMEM), (part_b, VMEM))
            + tuple((x, VMEM) for x in stats),
            ((wide_q, pltpu.VMEM(q_soft.shape, BF16), DMA((PARTS,))) if last else ())
            + (wide_kv,),
            flops=tile_flops,
            out_spec=HBM if last else VMEM,
        )
    soft_out = stats[0].reshape(tok, soft_heads, dim)

    befores = [jnp.zeros((count, dim, dim), BF16) for count in counts]
    arrived = [None] * HALVES
    for step in range(1, ranks - 1):
        for half in range(HALVES):
            if step > 1:
                befores[half] = befores[half] + arrived[half]
                moved = factors[half][:, None, :] * arrived[half].astype(F32)
                sends[half] = (moved + states[half]).astype(BF16)
            arrived[half] = lax.ppermute(sends[half], "ctx", [(step - 1, step)])

    intra, lin_query, lift = call(
        intra_body,
        (shaped((heads, tok, dim), F32), per_head, shaped((heads, tok, dim), F32)),
        ((q_lin_here, VMEM), (k_heads, VMEM), (v_heads, VMEM), (rise, VMEM)),
        (wide_lin,),
        flops=4 * heads * tok * tok * dim,
    )
    result = ()
    for half in range(HALVES):
        last = half == HALVES - 1
        result = call(
            functools.partial(finish_body, half),
            ((shaped(q_lin.shape, BF16),) if last else ()) + (shaped(q_lin.shape, F32),),
            tuple(
                (x, VMEM)
                for x in (intra, lin_query, lift, befores[half], arrived[half]) + result
            ),
            (flat_lin, DMA((PARTS,))) if last else (),
            flops=2 * counts[half] * tok * dim * dim,
            out_spec=(HBM, VMEM) if last else VMEM,
            aliases={5: int(last)} if half else {},
        )
    lin_out = result[0]
    return (lin_out.reshape(tok, heads, dim), soft_out)


def solution(mesh):
    wide = P(("group", "ctx"), ("head", "sub"), None)

    return jax.shard_map(
        on_device,
        mesh=mesh,
        in_specs=(wide, wide, wide, P(("group", "ctx"), ("head", "sub")), wide, wide, wide, P("group")),
        out_specs=(wide, wide),
        check_vma=False,
    )
```

```python
import functools
import math

import jax
import jax.numpy as jnp
from jax import lax
from jax.experimental import pallas as pl
from jax.experimental.pallas import tpu as pltpu
from jax.sharding import PartitionSpec as P


F32 = jnp.float32
BF16 = jnp.bfloat16
MASKED = -1e30
LOG2E = 1.0 / math.log(2.0)
VMEM = pl.BlockSpec(memory_space=pltpu.VMEM)
SMEM = pl.BlockSpec(memory_space=pltpu.SMEM)
HBM = pl.BlockSpec(memory_space=pltpu.HBM)
DMA = pltpu.SemaphoreType.DMA
SHARE = 13
CUTS = (0, 4, 8)
HALVES = len(CUTS) - 1


def shaped(shape, dtype):
    return jax.ShapeDtypeStruct(shape, dtype)


def call(body, outs, ins, scratch=(), flops=0, out_spec=VMEM, aliases={}):
    moved = sum(math.prod(x.shape) * x.dtype.itemsize for x in list(outs) + [i for i, _ in ins])
    return pl.pallas_call(
        body,
        out_shape=tuple(outs),
        in_specs=[spec for _, spec in ins],
        out_specs=out_spec if isinstance(out_spec, tuple) else (out_spec,) * len(outs),
        scratch_shapes=list(scratch),
        input_output_aliases=aliases,
        cost_estimate=pl.CostEstimate(flops=flops, bytes_accessed=moved, transcendentals=0),
        compiler_params=pltpu.CompilerParams(vmem_limit_bytes=16 << 20),
    )(*[pltpu.with_memory_space_constraint(x, pltpu.HBM) if spec is HBM else x for x, spec in ins])


def doc_at(docs_ref, position):
    count = jnp.int32(0)
    for i in range(docs_ref.shape[0]):
        count += (docs_ref[i] <= position).astype(jnp.int32)
    return count


def rise_of(decay_t):
    tok = decay_t.shape[1]
    rows = lax.broadcasted_iota(jnp.int32, (tok, tok), 0)
    columns = lax.broadcasted_iota(jnp.int32, (tok, tok), 1)
    upper = (rows <= columns).astype(F32)
    return jnp.dot(decay_t, upper, precision=lax.Precision.HIGHEST, preferred_element_type=F32)


def dot_t(a, b):
    return lax.dot_general(a, b, (((1,), (1,)), ((), ())), preferred_element_type=F32)


def dot(a, b):
    return jnp.dot(a, b, preferred_element_type=F32)


def pack_body(ranks, me_ref, k_hbm, v_hbm, *rest):
    parts, sems = (rest[:-1], rest[-1])

    @pl.when(me_ref[0] < ranks - 2)
    def _():
        rows = k_hbm.shape[0]
        copies = []
        first = 0
        for part in parts:
            end = first + part.shape[0]
            for i, x in enumerate((k_hbm, v_hbm)):
                low, high = (max(first, i * rows), min(end, (i + 1) * rows))
                if low < high:
                    copies.append(
                        pltpu.make_async_copy(
                            x.at[pl.ds(low - i * rows, high - low)],
                            part.at[pl.ds(low - first, high - low)],
                            sems.at[len(copies)],
                        )
                    )
            first = end
        for copy in copies:
            copy.start()
        for copy in copies:
            copy.wait()


def load_body(me_ref, docs_hbm, a_hbm, k_hbm, v_hbm, *rest):
    later = (len(rest) - 12) // 2
    fetched, (kh_ref, vh_ref, rise_ref, flags_ref), placed = (
        rest[:later],
        rest[later : later + 4],
        rest[later + 4 : 2 * later + 4],
    )
    docs, ab, kb, vb, kw, vw, sems, later_sems = rest[2 * later + 4 :]
    heads, tok, _ = kh_ref.shape
    copies = start_all((docs_hbm, a_hbm, k_hbm, v_hbm), (docs, ab, kb, vb), sems)
    extra = start_all(fetched, placed, later_sems)
    copies[0].wait()
    here = me_ref[0]
    doc = doc_at(docs, here * tok)
    keep = doc == doc_at(docs, (here + 1) * tok)
    flags_ref[0:1] = jnp.full((1, 128), jnp.where(keep, 1.0, 0.0), F32)
    for step in range(1, flags_ref.shape[0]):
        seen = (here >= step) & (doc_at(docs, (here - step) * tok) == doc)
        flags_ref[step : step + 1] = jnp.full((1, 128), jnp.where(seen, 0.0, MASKED), F32)
    copies[1].wait()
    rise_ref[...] = rise_of(ab[...])
    for copy, narrow, wide, out in ((copies[2], kb, kw, kh_ref), (copies[3], vb, vw, vh_ref)):
        copy.wait()
        wide[...] = narrow[...].astype(F32)
        for h in range(heads):
            out[h] = wide[pl.ds(h, tok, stride=heads), :].astype(BF16)
    for copy in extra:
        copy.wait()


def start_all(sources, targets, sems):
    copies = [
        pltpu.make_async_copy(src, dst, sems.at[i])
        for i, (src, dst) in enumerate(zip(sources, targets))
    ]
    for copy in copies:
        copy.start()
    return copies


def state_body(flags_ref, rise_ref, kh_ref, vh_ref, *outs):
    heads, tok, _ = kh_ref.shape
    states, sends, factors = (outs[:HALVES], outs[HALVES : 2 * HALVES], outs[2 * HALVES :])
    keep = flags_ref[0:1, :]
    rise = rise_ref[...]
    last = rise[:, tok - 1 : tok]
    factor = jnp.broadcast_to(jnp.exp(last), (heads, 128)) * keep
    fade = jnp.exp(last - rise)
    for half in range(HALVES):
        first, size = group_of(half, heads)
        factors[half][...] = factor[first : first + size]
        for i in range(size):
            h = first + i
            tail_t = (jnp.transpose(kh_ref[h].astype(F32)) * fade[h : h + 1, :]).astype(BF16)
            state = dot(tail_t, vh_ref[h]) * keep
            states[half][i] = state
            sends[half][i] = state.astype(BF16)


def intra_body(q_ref, kh_ref, vh_ref, rise_ref, intra_ref, qh_ref, lift_ref, qw):
    heads, tok, dim = kh_ref.shape
    rise_t = rise_ref[...] * LOG2E
    rise = jnp.transpose(rise_t)
    qw[...] = q_ref[...].astype(F32)
    half = tok // 2
    lower = lax.broadcasted_iota(jnp.int32, (half, half), 0) >= lax.broadcasted_iota(
        jnp.int32, (half, half), 1
    )
    for h in range(heads):
        query = qw[pl.ds(h, tok, stride=heads), :].astype(BF16)
        qh_ref[h] = query
        key, value = (kh_ref[h], vh_ref[h])
        column = jnp.broadcast_to(rise[:, h : h + 1], (tok, dim))
        lift_ref[h] = jnp.exp2(column)
        row = rise_t[h : h + 1, :]
        for part in range(2):
            low, high = (part * half, (part + 1) * half)
            scores = dot_t(query[low:high], key[:high])
            side = column[low:high, :half]
            end = jnp.exp2(jnp.where(lower, side - row[:, low:high], MASKED))
            fade = jnp.concatenate([jnp.exp2(side - row[:, :low]), end], axis=1) if part else end
            intra_ref[h, low:high] = dot((scores * fade).astype(BF16), value[:high])


def put_out(wide, narrow, out_hbm, sem, part, parts, pick=lambda x, here: x):
    rows = wide.shape[0] // parts
    here = pl.ds(part * rows, rows)
    narrow[here] = pick(wide[here], here).astype(BF16)
    copy = pltpu.make_async_copy(narrow.at[here], out_hbm.at[here], sem.at[part])
    copy.start()
    return copy


PARTS = 2


def group_of(half, heads):
    low, high = (CUTS[half] * heads // 8, CUTS[half + 1] * heads // 8)
    return low, high - low


def finish_body(half, intra_ref, qh_ref, lift_ref, before_ref, arrived_ref, *rest):
    heads, tok, dim = qh_ref.shape
    first, count = group_of(half, heads)
    last = half == HALVES - 1
    wide = rest[-3] if last else rest[-1]

    def pick(rows, here):
        if not half:
            return rows
        head = lax.broadcasted_iota(jnp.int32, rows.shape, 0) % heads
        return jnp.where(head < first, rest[0][here], rows)

    ones = jnp.full((dim, dim), 1.0, BF16)
    size = tok // PARTS
    copies = []
    for part in range(PARTS):
        rows = pl.ds(part * size, size)
        for i in range(count):
            h = first + i
            inter = dot(qh_ref[h, rows], before_ref[i] + arrived_ref[i])
            total = intra_ref[h, rows] + lift_ref[h, rows] * inter
            mean = dot((total * total).astype(BF16), ones) * (1.0 / dim)
            wide[pl.ds(part * size * heads + h, size, stride=heads), :] = total * lax.rsqrt(
                mean + 1e-06
            )
        if last:
            copies.append(put_out(wide, rest[-2], rest[-4], rest[-1], part, PARTS, pick))
    if not last and half:
        wide[...] = pick(wide[...], slice(None))
    for copy in copies:
        copy.wait()


def sides_of(parts, wide, count):
    first = 0
    for part in parts:
        wide[first : first + part.shape[0]] = part[...].astype(F32)
        first += part.shape[0]
    keys = first // (2 * count)
    ones = jnp.ones((keys, 128), BF16)
    sides = []
    for g in range(count):
        key, value = (
            wide[pl.ds(side * (first // 2) + g, keys, stride=count), :].astype(BF16)
            for side in range(2)
        )
        sides.append((key, jnp.concatenate([value, ones], axis=1)))
    return sides


def first_tile_body(kv_heads, heads, q_ref, k_ref, v_ref, qh_ref, top_ref, acc_ref, qw, kvw):
    tok = q_ref.shape[0] // heads
    power = LOG2E / math.sqrt(q_ref.shape[1])
    half = tok // 2
    lower = lax.broadcasted_iota(jnp.int32, (half, half), 0) >= lax.broadcasted_iota(
        jnp.int32, (half, half), 1
    )
    qw[...] = q_ref[...].astype(F32)
    for g, (key, value) in enumerate(sides_of((k_ref, v_ref), kvw, kv_heads)):
        for h in range(g * heads // kv_heads, (g + 1) * heads // kv_heads):
            query = qw[pl.ds(h, tok, stride=heads), :].astype(BF16)
            qh_ref[h] = query
            for part in range(2):
                low, high = (part * half, (part + 1) * half)
                scores = dot_t(query[low:high], key[:high])
                end = jnp.where(lower, scores[:, low:], MASKED)
                scores = jnp.concatenate([scores[:, :low], end], axis=1) if part else end
                top = jnp.max(scores, axis=-1, keepdims=True)
                weights = jnp.exp2((scores - top) * power).astype(BF16)
                top_ref[h, low:high] = jnp.broadcast_to(top, (half, 128))
                acc_ref[h, low:high] = dot(weights, value[:high])


def next_tile_body(
    kv_heads, step, last, me_ref, flags_ref, qh_ref, a_ref, b_ref, top_ref, acc_ref, *rest
):
    heads, tok, dim = qh_ref.shape
    power = LOG2E / math.sqrt(dim)
    parts = PARTS if last else 2
    size = tok // parts

    def put(part, h, acc, summed):
        rest[1][pl.ds(part * size * heads + h, size, stride=heads), :] = acc / summed

    @pl.when(me_ref[0] >= step)
    def _():
        bias = flags_ref[step : step + 1, :]
        sides = sides_of((a_ref, b_ref), rest[-1], kv_heads)
        copies = []
        for part in range(parts):
            rows = pl.ds(part * size, size)
            for h in range(heads):
                key, value = sides[h * kv_heads // heads]
                scores = dot_t(qh_ref[h, rows], key)
                old = top_ref[h, rows]
                top = jnp.max(scores, axis=-1, keepdims=True) + bias
                new = jnp.maximum(old, top)
                shift = jnp.tile(new - bias, (1, tok // 128))
                weights = jnp.exp2((scores - shift) * power).astype(BF16)
                shrink = jnp.exp2((old - new) * power)
                both = dot(weights, value)
                acc = acc_ref[h, rows, :dim] * shrink + both[:, :dim]
                summed = acc_ref[h, rows, dim:] * shrink + both[:, dim:]
                if last:
                    put(part, h, acc, summed)
                else:
                    rest[0][h, rows] = new
                    rest[1][h, rows, :dim] = acc
                    rest[1][h, rows, dim:] = summed
            if last:
                copies.append(put_out(rest[1], rest[2], rest[0], rest[3], part, parts))
        for copy in copies:
            copy.wait()

    @pl.when(me_ref[0] < step)
    def _():
        if last:
            copies = []
            for part in range(parts):
                rows = pl.ds(part * size, size)
                for h in range(heads):
                    put(part, h, acc_ref[h, rows, :dim], acc_ref[h, rows, dim:])
                copies.append(put_out(rest[1], rest[2], rest[0], rest[3], part, parts))
            for copy in copies:
                copy.wait()
        else:
            rest[0][...] = top_ref[...]
            rest[1][...] = acc_ref[...]


def on_device(q_lin, k_lin, v_lin, decay_log, q_soft, k_soft, v_soft, doc_starts):
    tok, heads, dim = q_lin.shape
    soft_heads, kv_heads = (q_soft.shape[1], k_soft.shape[1])
    ranks = lax.axis_size("ctx")
    me = lax.axis_index("ctx")[None]
    flat = lambda x: x.reshape(-1, dim)
    q_lin, k_lin, v_lin, q_soft, k_soft, v_soft = map(
        flat, (q_lin, k_lin, v_lin, q_soft, k_soft, v_soft)
    )
    decay_t = decay_log.T
    wide_lin = pltpu.VMEM(q_lin.shape, F32)
    wide_q = pltpu.VMEM(q_soft.shape, F32)
    wide_kv = pltpu.VMEM((2 * k_soft.shape[0], dim), F32)
    flat_lin = pltpu.VMEM(q_lin.shape, BF16)
    per_head = shaped((heads, tok, dim), BF16)

    fetched = (q_lin, q_soft, k_soft, v_soft)
    total = 2 * k_soft.shape[0]
    early = total * SHARE // 32
    part_a, part_b = call(
        functools.partial(pack_body, ranks),
        (shaped((early, dim), BF16), shaped((total - early, dim), BF16)),
        ((me, SMEM), (k_soft, HBM), (v_soft, HBM)),
        (DMA((4,)),),
    )
    k_heads, v_heads, rise, flags, q_lin_here, q_here, k_here, v_here = call(
        load_body,
        (
            per_head,
            per_head,
            shaped((heads, tok), F32),
            shaped((ranks, 128), F32),
        )
        + tuple(shaped(x.shape, x.dtype) for x in fetched),
        ((me, SMEM),)
        + tuple((x, HBM) for x in (doc_starts, decay_t, k_lin, v_lin) + fetched),
        (
            pltpu.SMEM(doc_starts.shape, jnp.int32),
            pltpu.VMEM((heads, tok), F32),
            flat_lin,
            flat_lin,
            wide_lin,
            wide_lin,
            DMA((4,)),
            DMA((len(fetched),)),
        ),
    )
    counts = [group_of(half, heads)[1] for half in range(HALVES)]
    outs = call(
        state_body,
        tuple(shaped((count, dim, dim), F32) for count in counts)
        + tuple(shaped((count, dim, dim), BF16) for count in counts)
        + tuple(shaped((count, 128), F32) for count in counts),
        ((flags, VMEM), (rise, VMEM), (k_heads, VMEM), (v_heads, VMEM)),
        flops=2 * heads * tok * dim * dim,
    )
    states, sends, factors = (outs[:HALVES], list(outs[HALVES : 2 * HALVES]), outs[2 * HALVES :])
    tile_flops = 6 * soft_heads * tok * tok * dim
    stat_shapes = (shaped((soft_heads, tok, 128), F32), shaped((soft_heads, tok, 2 * dim), F32))
    soft_query, *stats = call(
        functools.partial(first_tile_body, kv_heads, soft_heads),
        (shaped((soft_heads, tok, dim), BF16),) + stat_shapes,
        ((q_here, VMEM), (k_here, VMEM), (v_here, VMEM)),
        (wide_q, wide_kv),
        flops=tile_flops,
    )
    for step in range(1, ranks - 1):
        pairs = [(i, i + 1) for i in range(step - 1, ranks - 2)]
        part_a = lax.ppermute(part_a, "ctx", pairs)
        part_b = lax.ppermute(part_b, "ctx", pairs)
        last = step == ranks - 2
        stats = call(
            functools.partial(next_tile_body, kv_heads, step, last),
            (shaped(q_soft.shape, BF16),) if last else stat_shapes,
            ((me, SMEM), (flags, VMEM), (soft_query, VMEM), (part_a, VMEM), (part_b, VMEM))
            + tuple((x, VMEM) for x in stats),
            ((wide_q, pltpu.VMEM(q_soft.shape, BF16), DMA((PARTS,))) if last else ())
            + (wide_kv,),
            flops=tile_flops,
            out_spec=HBM if last else VMEM,
        )
    soft_out = stats[0].reshape(tok, soft_heads, dim)

    befores = [jnp.zeros((count, dim, dim), BF16) for count in counts]
    arrived = [None] * HALVES
    for step in range(1, ranks - 1):
        for half in range(HALVES):
            if step > 1:
                befores[half] = befores[half] + arrived[half]
                moved = factors[half][:, None, :] * arrived[half].astype(F32)
                sends[half] = (moved + states[half]).astype(BF16)
            arrived[half] = lax.ppermute(sends[half], "ctx", [(step - 1, step)])

    intra, lin_query, lift = call(
        intra_body,
        (shaped((heads, tok, dim), F32), per_head, shaped((heads, tok, dim), F32)),
        ((q_lin_here, VMEM), (k_heads, VMEM), (v_heads, VMEM), (rise, VMEM)),
        (wide_lin,),
        flops=4 * heads * tok * tok * dim,
    )
    result = ()
    for half in range(HALVES):
        last = half == HALVES - 1
        result = call(
            functools.partial(finish_body, half),
            (shaped(q_lin.shape, BF16 if last else F32),),
            tuple(
                (x, VMEM)
                for x in (intra, lin_query, lift, befores[half], arrived[half]) + result
            ),
            (wide_lin, flat_lin, DMA((PARTS,))) if last else (),
            flops=2 * counts[half] * tok * dim * dim,
            out_spec=HBM if last else VMEM,
        )
    lin_out = result[0]
    return (lin_out.reshape(tok, heads, dim), soft_out)


def solution(mesh):
    wide = P(("group", "ctx"), ("head", "sub"), None)

    return jax.shard_map(
        on_device,
        mesh=mesh,
        in_specs=(wide, wide, wide, P(("group", "ctx"), ("head", "sub")), wide, wide, wide, P("group")),
        out_specs=(wide, wide),
        check_vma=False,
    )
```

```python
import functools
import math

import jax
import jax.numpy as jnp
from jax import lax
from jax.experimental import pallas as pl
from jax.experimental.pallas import tpu as pltpu
from jax.sharding import PartitionSpec as P


F32 = jnp.float32
BF16 = jnp.bfloat16
MASKED = -1e30
LOG2E = 1.0 / math.log(2.0)
VMEM = pl.BlockSpec(memory_space=pltpu.VMEM)
SMEM = pl.BlockSpec(memory_space=pltpu.SMEM)
HBM = pl.BlockSpec(memory_space=pltpu.HBM)
DMA = pltpu.SemaphoreType.DMA
SHARE = 13
CUTS = (0, 4, 8)
HALVES = len(CUTS) - 1


def shaped(shape, dtype):
    return jax.ShapeDtypeStruct(shape, dtype)


def call(body, outs, ins, scratch=(), flops=0, out_spec=VMEM, aliases={}):
    moved = sum(math.prod(x.shape) * x.dtype.itemsize for x in list(outs) + [i for i, _ in ins])
    return pl.pallas_call(
        body,
        out_shape=tuple(outs),
        in_specs=[spec for _, spec in ins],
        out_specs=out_spec if isinstance(out_spec, tuple) else (out_spec,) * len(outs),
        scratch_shapes=list(scratch),
        input_output_aliases=aliases,
        cost_estimate=pl.CostEstimate(flops=flops, bytes_accessed=moved, transcendentals=0),
        compiler_params=pltpu.CompilerParams(vmem_limit_bytes=16 << 20),
    )(*[pltpu.with_memory_space_constraint(x, pltpu.HBM) if spec is HBM else x for x, spec in ins])


def doc_at(docs_ref, position):
    count = jnp.int32(0)
    for i in range(docs_ref.shape[0]):
        count += (docs_ref[i] <= position).astype(jnp.int32)
    return count


def rise_of(decay_t):
    tok = decay_t.shape[1]
    rows = lax.broadcasted_iota(jnp.int32, (tok, tok), 0)
    columns = lax.broadcasted_iota(jnp.int32, (tok, tok), 1)
    upper = (rows <= columns).astype(F32)
    return jnp.dot(decay_t, upper, precision=lax.Precision.HIGHEST, preferred_element_type=F32)


def dot_t(a, b):
    return lax.dot_general(a, b, (((1,), (1,)), ((), ())), preferred_element_type=F32)


def dot(a, b):
    return jnp.dot(a, b, preferred_element_type=F32)


def pack_body(ranks, me_ref, k_hbm, v_hbm, *rest):
    parts, sems = (rest[:-1], rest[-1])

    @pl.when(me_ref[0] < ranks - 2)
    def _():
        rows = k_hbm.shape[0]
        copies = []
        first = 0
        for part in parts:
            end = first + part.shape[0]
            for i, x in enumerate((k_hbm, v_hbm)):
                low, high = (max(first, i * rows), min(end, (i + 1) * rows))
                if low < high:
                    copies.append(
                        pltpu.make_async_copy(
                            x.at[pl.ds(low - i * rows, high - low)],
                            part.at[pl.ds(low - first, high - low)],
                            sems.at[len(copies)],
                        )
                    )
            first = end
        for copy in copies:
            copy.start()
        for copy in copies:
            copy.wait()


def load_body(me_ref, docs_hbm, a_hbm, k_hbm, v_hbm, *rest):
    later = (len(rest) - 12) // 2
    fetched, (kh_ref, vh_ref, rise_ref, flags_ref), placed = (
        rest[:later],
        rest[later : later + 4],
        rest[later + 4 : 2 * later + 4],
    )
    docs, ab, kb, vb, kw, vw, sems, later_sems = rest[2 * later + 4 :]
    heads, tok, _ = kh_ref.shape
    copies = start_all((docs_hbm, a_hbm, k_hbm, v_hbm), (docs, ab, kb, vb), sems)
    extra = start_all(fetched, placed, later_sems)
    copies[0].wait()
    here = me_ref[0]
    doc = doc_at(docs, here * tok)
    keep = doc == doc_at(docs, (here + 1) * tok)
    flags_ref[0:1] = jnp.full((1, 128), jnp.where(keep, 1.0, 0.0), F32)
    for step in range(1, flags_ref.shape[0]):
        seen = (here >= step) & (doc_at(docs, (here - step) * tok) == doc)
        flags_ref[step : step + 1] = jnp.full((1, 128), jnp.where(seen, 0.0, MASKED), F32)
    copies[1].wait()
    rise_ref[...] = rise_of(ab[...])
    for copy, narrow, wide, out in ((copies[2], kb, kw, kh_ref), (copies[3], vb, vw, vh_ref)):
        copy.wait()
        wide[...] = narrow[...].astype(F32)
        for h in range(heads):
            out[h] = wide[pl.ds(h, tok, stride=heads), :].astype(BF16)
    for copy in extra:
        copy.wait()


def start_all(sources, targets, sems):
    copies = [
        pltpu.make_async_copy(src, dst, sems.at[i])
        for i, (src, dst) in enumerate(zip(sources, targets))
    ]
    for copy in copies:
        copy.start()
    return copies


def state_body(flags_ref, rise_ref, kh_ref, vh_ref, *outs):
    heads, tok, _ = kh_ref.shape
    states, sends, factors = (outs[:HALVES], outs[HALVES : 2 * HALVES], outs[2 * HALVES :])
    keep = flags_ref[0:1, :]
    rise = rise_ref[...]
    last = rise[:, tok - 1 : tok]
    factor = jnp.broadcast_to(jnp.exp(last), (heads, 128)) * keep
    fade = jnp.exp(last - rise)
    for half in range(HALVES):
        first, size = group_of(half, heads)
        factors[half][...] = factor[first : first + size]
        for i in range(size):
            h = first + i
            tail_t = (jnp.transpose(kh_ref[h].astype(F32)) * fade[h : h + 1, :]).astype(BF16)
            state = dot(tail_t, vh_ref[h]) * keep
            states[half][i] = state
            sends[half][i] = state.astype(BF16)


def intra_body(q_ref, kh_ref, vh_ref, rise_ref, intra_ref, qh_ref, lift_ref, qw):
    heads, tok, dim = kh_ref.shape
    rise_t = rise_ref[...] * LOG2E
    rise = jnp.transpose(rise_t)
    qw[...] = q_ref[...].astype(F32)
    half = tok // 2
    lower = lax.broadcasted_iota(jnp.int32, (half, half), 0) >= lax.broadcasted_iota(
        jnp.int32, (half, half), 1
    )
    for h in range(heads):
        query = qw[pl.ds(h, tok, stride=heads), :].astype(BF16)
        qh_ref[h] = query
        key, value = (kh_ref[h], vh_ref[h])
        column = jnp.broadcast_to(rise[:, h : h + 1], (tok, dim))
        lift_ref[h] = jnp.exp2(column)
        row = rise_t[h : h + 1, :]
        for part in range(2):
            low, high = (part * half, (part + 1) * half)
            scores = dot_t(query[low:high], key[:high])
            side = column[low:high, :half]
            end = jnp.exp2(jnp.where(lower, side - row[:, low:high], MASKED))
            fade = jnp.concatenate([jnp.exp2(side - row[:, :low]), end], axis=1) if part else end
            intra_ref[h, low:high] = dot((scores * fade).astype(BF16), value[:high])


def put_out(wide, narrow, out_hbm, sem, part, parts, pick=lambda x, here: x):
    rows = wide.shape[0] // parts
    here = pl.ds(part * rows, rows)
    narrow[here] = pick(wide[here], here).astype(BF16)
    copy = pltpu.make_async_copy(narrow.at[here], out_hbm.at[here], sem.at[part])
    copy.start()
    return copy


PARTS = 2


def group_of(half, heads):
    low, high = (CUTS[half] * heads // 8, CUTS[half + 1] * heads // 8)
    return low, high - low


def finish_body(half, intra_ref, qh_ref, lift_ref, before_ref, arrived_ref, *rest):
    heads, tok, dim = qh_ref.shape
    first, count = group_of(half, heads)
    last = half == HALVES - 1
    wide = rest[-3] if last else rest[-1]

    def pick(rows, here):
        if not half:
            return rows
        head = lax.broadcasted_iota(jnp.int32, rows.shape, 0) % heads
        return jnp.where(head < first, rest[0][here], rows)

    ones = jnp.full((dim, dim), 1.0, BF16)
    for i in range(count):
        h = first + i
        inter = dot(qh_ref[h], before_ref[i] + arrived_ref[i])
        total = intra_ref[h] + lift_ref[h] * inter
        mean = dot((total * total).astype(BF16), ones) * (1.0 / dim)
        wide[pl.ds(h, tok, stride=heads), :] = total * lax.rsqrt(mean + 1e-06)
    copies = []
    if last:
        for part in range(PARTS):
            copies.append(put_out(wide, rest[-2], rest[-4], rest[-1], part, PARTS, pick))
    if not last and half:
        wide[...] = pick(wide[...], slice(None))
    for copy in copies:
        copy.wait()


def sides_of(parts, wide, count):
    first = 0
    for part in parts:
        wide[first : first + part.shape[0]] = part[...].astype(F32)
        first += part.shape[0]
    keys = first // (2 * count)
    ones = jnp.ones((keys, 128), BF16)
    sides = []
    for g in range(count):
        key, value = (
            wide[pl.ds(side * (first // 2) + g, keys, stride=count), :].astype(BF16)
            for side in range(2)
        )
        sides.append((key, jnp.concatenate([value, ones], axis=1)))
    return sides


def first_tile_body(kv_heads, heads, q_ref, k_ref, v_ref, qh_ref, top_ref, acc_ref, qw, kvw):
    tok = q_ref.shape[0] // heads
    power = LOG2E / math.sqrt(q_ref.shape[1])
    half = tok // 2
    lower = lax.broadcasted_iota(jnp.int32, (half, half), 0) >= lax.broadcasted_iota(
        jnp.int32, (half, half), 1
    )
    qw[...] = q_ref[...].astype(F32)
    for g, (key, value) in enumerate(sides_of((k_ref, v_ref), kvw, kv_heads)):
        for h in range(g * heads // kv_heads, (g + 1) * heads // kv_heads):
            query = qw[pl.ds(h, tok, stride=heads), :].astype(BF16)
            qh_ref[h] = query
            for part in range(2):
                low, high = (part * half, (part + 1) * half)
                scores = dot_t(query[low:high], key[:high])
                end = jnp.where(lower, scores[:, low:], MASKED)
                scores = jnp.concatenate([scores[:, :low], end], axis=1) if part else end
                top = jnp.max(scores, axis=-1, keepdims=True)
                weights = jnp.exp2((scores - top) * power).astype(BF16)
                top_ref[h, low:high] = jnp.broadcast_to(top, (half, 128))
                acc_ref[h, low:high] = dot(weights, value[:high])


def next_tile_body(
    kv_heads, step, last, me_ref, flags_ref, qh_ref, a_ref, b_ref, top_ref, acc_ref, *rest
):
    heads, tok, dim = qh_ref.shape
    power = LOG2E / math.sqrt(dim)
    parts = PARTS if last else 2
    size = tok // parts

    def put(part, h, acc, summed):
        rest[1][pl.ds(part * size * heads + h, size, stride=heads), :] = acc / summed

    @pl.when(me_ref[0] >= step)
    def _():
        bias = flags_ref[step : step + 1, :]
        sides = sides_of((a_ref, b_ref), rest[-1], kv_heads)
        copies = []
        for part in range(parts):
            rows = pl.ds(part * size, size)
            for h in range(heads):
                key, value = sides[h * kv_heads // heads]
                scores = dot_t(qh_ref[h, rows], key)
                old = top_ref[h, rows]
                top = jnp.max(scores, axis=-1, keepdims=True) + bias
                new = jnp.maximum(old, top)
                shift = jnp.tile(new - bias, (1, tok // 128))
                weights = jnp.exp2((scores - shift) * power).astype(BF16)
                shrink = jnp.exp2((old - new) * power)
                both = dot(weights, value)
                acc = acc_ref[h, rows, :dim] * shrink + both[:, :dim]
                summed = acc_ref[h, rows, dim:] * shrink + both[:, dim:]
                if last:
                    put(part, h, acc, summed)
                else:
                    rest[0][h, rows] = new
                    rest[1][h, rows, :dim] = acc
                    rest[1][h, rows, dim:] = summed
            if last:
                copies.append(put_out(rest[1], rest[2], rest[0], rest[3], part, parts))
        for copy in copies:
            copy.wait()

    @pl.when(me_ref[0] < step)
    def _():
        if last:
            copies = []
            for part in range(parts):
                rows = pl.ds(part * size, size)
                for h in range(heads):
                    put(part, h, acc_ref[h, rows, :dim], acc_ref[h, rows, dim:])
                copies.append(put_out(rest[1], rest[2], rest[0], rest[3], part, parts))
            for copy in copies:
                copy.wait()
        else:
            rest[0][...] = top_ref[...]
            rest[1][...] = acc_ref[...]


def on_device(q_lin, k_lin, v_lin, decay_log, q_soft, k_soft, v_soft, doc_starts):
    tok, heads, dim = q_lin.shape
    soft_heads, kv_heads = (q_soft.shape[1], k_soft.shape[1])
    ranks = lax.axis_size("ctx")
    me = lax.axis_index("ctx")[None]
    flat = lambda x: x.reshape(-1, dim)
    q_lin, k_lin, v_lin, q_soft, k_soft, v_soft = map(
        flat, (q_lin, k_lin, v_lin, q_soft, k_soft, v_soft)
    )
    decay_t = decay_log.T
    wide_lin = pltpu.VMEM(q_lin.shape, F32)
    wide_q = pltpu.VMEM(q_soft.shape, F32)
    wide_kv = pltpu.VMEM((2 * k_soft.shape[0], dim), F32)
    flat_lin = pltpu.VMEM(q_lin.shape, BF16)
    per_head = shaped((heads, tok, dim), BF16)

    fetched = (q_lin, q_soft, k_soft, v_soft)
    total = 2 * k_soft.shape[0]
    early = total * SHARE // 32
    part_a, part_b = call(
        functools.partial(pack_body, ranks),
        (shaped((early, dim), BF16), shaped((total - early, dim), BF16)),
        ((me, SMEM), (k_soft, HBM), (v_soft, HBM)),
        (DMA((4,)),),
    )
    k_heads, v_heads, rise, flags, q_lin_here, q_here, k_here, v_here = call(
        load_body,
        (
            per_head,
            per_head,
            shaped((heads, tok), F32),
            shaped((ranks, 128), F32),
        )
        + tuple(shaped(x.shape, x.dtype) for x in fetched),
        ((me, SMEM),)
        + tuple((x, HBM) for x in (doc_starts, decay_t, k_lin, v_lin) + fetched),
        (
            pltpu.SMEM(doc_starts.shape, jnp.int32),
            pltpu.VMEM((heads, tok), F32),
            flat_lin,
            flat_lin,
            wide_lin,
            wide_lin,
            DMA((4,)),
            DMA((len(fetched),)),
        ),
    )
    counts = [group_of(half, heads)[1] for half in range(HALVES)]
    outs = call(
        state_body,
        tuple(shaped((count, dim, dim), F32) for count in counts)
        + tuple(shaped((count, dim, dim), BF16) for count in counts)
        + tuple(shaped((count, 128), F32) for count in counts),
        ((flags, VMEM), (rise, VMEM), (k_heads, VMEM), (v_heads, VMEM)),
        flops=2 * heads * tok * dim * dim,
    )
    states, sends, factors = (outs[:HALVES], list(outs[HALVES : 2 * HALVES]), outs[2 * HALVES :])
    tile_flops = 6 * soft_heads * tok * tok * dim
    stat_shapes = (shaped((soft_heads, tok, 128), F32), shaped((soft_heads, tok, 2 * dim), F32))
    soft_query, *stats = call(
        functools.partial(first_tile_body, kv_heads, soft_heads),
        (shaped((soft_heads, tok, dim), BF16),) + stat_shapes,
        ((q_here, VMEM), (k_here, VMEM), (v_here, VMEM)),
        (wide_q, wide_kv),
        flops=tile_flops,
    )
    for step in range(1, ranks - 1):
        pairs = [(i, i + 1) for i in range(step - 1, ranks - 2)]
        part_a = lax.ppermute(part_a, "ctx", pairs)
        part_b = lax.ppermute(part_b, "ctx", pairs)
        last = step == ranks - 2
        stats = call(
            functools.partial(next_tile_body, kv_heads, step, last),
            (shaped(q_soft.shape, BF16),) if last else stat_shapes,
            ((me, SMEM), (flags, VMEM), (soft_query, VMEM), (part_a, VMEM), (part_b, VMEM))
            + tuple((x, VMEM) for x in stats),
            ((wide_q, pltpu.VMEM(q_soft.shape, BF16), DMA((PARTS,))) if last else ())
            + (wide_kv,),
            flops=tile_flops,
            out_spec=HBM if last else VMEM,
        )
    soft_out = stats[0].reshape(tok, soft_heads, dim)

    befores = [jnp.zeros((count, dim, dim), BF16) for count in counts]
    arrived = [None] * HALVES
    for step in range(1, ranks - 1):
        for half in range(HALVES):
            if step > 1:
                befores[half] = befores[half] + arrived[half]
                moved = factors[half][:, None, :] * arrived[half].astype(F32)
                sends[half] = (moved + states[half]).astype(BF16)
            arrived[half] = lax.ppermute(sends[half], "ctx", [(step - 1, step)])

    intra, lin_query, lift = call(
        intra_body,
        (shaped((heads, tok, dim), F32), per_head, shaped((heads, tok, dim), F32)),
        ((q_lin_here, VMEM), (k_heads, VMEM), (v_heads, VMEM), (rise, VMEM)),
        (wide_lin,),
        flops=4 * heads * tok * tok * dim,
    )
    result = ()
    for half in range(HALVES):
        last = half == HALVES - 1
        result = call(
            functools.partial(finish_body, half),
            (shaped(q_lin.shape, BF16 if last else F32),),
            tuple(
                (x, VMEM)
                for x in (intra, lin_query, lift, befores[half], arrived[half]) + result
            ),
            (wide_lin, flat_lin, DMA((PARTS,))) if last else (),
            flops=2 * counts[half] * tok * dim * dim,
            out_spec=HBM if last else VMEM,
        )
    lin_out = result[0]
    return (lin_out.reshape(tok, heads, dim), soft_out)


def solution(mesh):
    wide = P(("group", "ctx"), ("head", "sub"), None)

    return jax.shard_map(
        on_device,
        mesh=mesh,
        in_specs=(wide, wide, wide, P(("group", "ctx"), ("head", "sub")), wide, wide, wide, P("group")),
        out_specs=(wide, wide),
        check_vma=False,
    )
```
